256 devices in a mesh: ctx: 32 (over z_hi, x, core), tp: 8 (over y, z_lo).
Axes of the slice: x: 4, y: 4, z: 8 (z_hi: 4, z_lo: 2; z = z_hi * 2 + z_lo), core: 2. Of those that a mesh axis runs over, the one named last changes fastest.
Arguments:
- features: bfloat16 [16384, 3, 4096], P('ctx', None, 'tp'), may hold values from -6 to 6
- short_filter: float32 [3, 7, 4096], P(None, None, 'tp'), may hold values from -2 to 2
- decay_rate: float32 [16, 4096], P(None, 'tp'), may hold values from 0 to 1, as said below
- residue: float32 [16, 4096], P(None, 'tp'), may hold values from -2 to 2
- skip_gain: float32 [4096], P('tp'), may hold values from -4 to 4
- norm_gain: float32 [4096], replicated, may hold values from 0.1 to 1.9
- qkv_weight: bfloat16 [4096, 3, 2048], P('ctx', None, 'tp'), may hold values from -2 to 2
Outputs:
- mixer: bfloat16 [16384, 4096], P('ctx', 'tp')
- attended: bfloat16 [16384, 2048], P('ctx', 'tp')
The draws below stay inside these ranges and needn't reach their ends.
Inputs may be any that keep to these rules, and one draw needn't show every extreme that they name: `decay_rate`: decay rates are positive.
All inputs are finite; a program needn't handle non-finite values.
Results may differ from the reference program's by a relative error of at most 0.01.
Values may be sent and summed in bfloat16 or wider, within the bound.
No kernel may reach another device: no remote copies, remote signals or barrier semaphores. Data moves between devices by JAX's collectives and lax.ppermute only.
A program may use at most 128 MiB of HBM per device.

```python
import math
import jax
import jax.numpy as jnp
from jax import lax

D = 4096
HD = 128
HEADS = 16
NMODES = 16
TAPS = 7
WINDOW = 3
TOK_DEV = 512
TOKENS = 16384
N_CTX = 32


def draw_decay_rate(key, part):
    lowest = math.log(0.1 / TOKENS)
    highest = math.log(1.0 / 30.0)
    unit = jax.random.uniform(jax.random.fold_in(key, 11), (NMODES, D), jnp.float32)
    return jnp.exp(lowest + unit * (highest - lowest))


def draw_qkv_weight(key, part):
    base = jax.random.truncated_normal(jax.random.fold_in(key, 21), -4.0, 4.0, (D, 3, HEADS, HD), jnp.float32) * D ** (-0.5)
    return base.reshape(D, 3, HEADS * HD).astype(jnp.bfloat16)


def level_of(own_key, shape, cuts, low, high):
    level, own = 1.0, jax.random.fold_in(own_key, 6)
    for axis_at, shards_of in cuts:
        draws = jnp.exp(jax.random.uniform(jax.random.fold_in(own, axis_at), (shards_of,), jnp.float32, low / len(cuts), high / len(cuts)))
        level = level * jnp.repeat(draws, shape[axis_at] // shards_of).reshape([-1 if axis == axis_at else 1 for axis in range(len(shape))])
    return level


def centred(stream_key, dims, spread, bound, split=(), kind=jnp.bfloat16):
    values = spread * jax.random.normal(stream_key, dims, jnp.float32)
    if split:
        values = values * level_of(stream_key, dims, split, -0.22, 0.18)
    return jnp.clip(values, -bound, bound).astype(kind)


def setup_inputs(seed: int = 0) -> dict:
    key_of = jax.random.split(jax.random.key(seed), 8)
    features = centred(key_of[0], (TOKENS, 3, D), 1.0, 6.0, ((0, 32), (2, 8)))
    short_filter = centred(key_of[1], (3, TAPS, D), TAPS ** -0.5, 2.0, ((2, 8),), jnp.float32)
    decay_rate = draw_decay_rate(jax.random.fold_in(key_of[7], 71), 0)
    residue = centred(key_of[3], (NMODES, D), 0.35, 2.0, ((1, 8),), jnp.float32)
    skip_gain = centred(key_of[4], (D,), 1.0, 4.0, ((0, 8),), jnp.float32)
    norm_gain = jnp.clip(1.0 + 0.18 * jax.random.normal(key_of[5], (D,), jnp.float32), 0.1, 1.9)
    qkv_weight = draw_qkv_weight(jax.random.fold_in(key_of[7], 71), 0)
    return dict(features=features, short_filter=short_filter, decay_rate=decay_rate, residue=residue, skip_gain=skip_gain, norm_gain=norm_gain, qkv_weight=qkv_weight)


EPSILON = 1e-06

def hyena_group(feat_group, taps_group, decay_group, residue_group, skip_group):
    as_float = feat_group.astype(jnp.float32)
    padded = jnp.pad(as_float, ((TAPS - 1, 0), (0, 0), (0, 0)))
    short = jnp.zeros_like(as_float)
    for offset in range(TAPS):
        first_row = TAPS - 1 - offset
        short = short + taps_group[:, offset, :][None] * padded[first_row:first_row + TOKENS]
    gated = lax.optimization_barrier((short[:, 1] * short[:, 2]).astype(jnp.bfloat16)).astype(jnp.float32)
    channels = feat_group.shape[2]
    lag_values = jnp.arange(TOKENS).astype(jnp.float32)
    kernel = jnp.zeros((channels, TOKENS), jnp.float32)
    for mode in range(NMODES):
        mode_weight = residue_group[mode] * jnp.sqrt(decay_group[mode])
        kernel = kernel + mode_weight[:, None] * jnp.exp(-decay_group[mode][:, None] * lag_values[None, :])
    length = 2 * TOKENS
    spectrum = jnp.fft.rfft(gated.T, n=length) * jnp.fft.rfft(kernel, n=length)
    filtered = jnp.fft.irfft(spectrum, n=length)[:, :TOKENS].T + skip_group[None] * gated
    filtered = lax.optimization_barrier(filtered.astype(jnp.bfloat16)).astype(jnp.float32)
    return (short[:, 0] * filtered).astype(jnp.bfloat16)

def reference(features, short_filter, decay_rate, residue, skip_gain, norm_gain, qkv_weight):
    group = 128 if D % 128 == 0 else D
    count = D // group
    feats = features.reshape(TOKENS, 3, count, group).transpose(2, 0, 1, 3)
    taps = short_filter.reshape(3, TAPS, count, group).transpose(2, 0, 1, 3)
    decays = decay_rate.reshape(NMODES, count, group).transpose(1, 0, 2)
    residues = residue.reshape(NMODES, count, group).transpose(1, 0, 2)
    skips = skip_gain.reshape(count, group)
    pieces = lax.map(lambda items: hyena_group(*items), (feats, taps, decays, residues, skips))
    mixer = pieces.transpose(1, 0, 2).reshape(TOKENS, D)
    head_cols = HEADS * HD
    weight_flat = qkv_weight.reshape(D, 3 * head_cols)

    def project(block):
        as_float = block.astype(jnp.float32)
        inverse = lax.rsqrt(lax.optimization_barrier(jnp.mean(as_float * as_float, axis=1, keepdims=True)) + EPSILON)
        normed = (as_float * inverse * norm_gain[None]).astype(jnp.bfloat16)
        return jnp.dot(normed, weight_flat, preferred_element_type=jnp.float32).astype(jnp.bfloat16)
    projected = lax.map(project, mixer.reshape(N_CTX, TOK_DEV, D))
    projected = projected.reshape(TOKENS, 3, HEADS, HD)
    queries = projected[:, 0].reshape(N_CTX, TOK_DEV, HEADS, HD)
    key_values = jnp.pad(projected[:, 1:3], (((WINDOW - 1) * TOK_DEV, 0), (0, 0), (0, 0), (0, 0)))

    def attend(items):
        index, query = items
        first_row = (index * TOK_DEV).astype(jnp.int32)
        window_kv = lax.dynamic_slice_in_dim(key_values, first_row, WINDOW * TOK_DEV, 0)
        keys = window_kv[:, 0].astype(jnp.float32)
        values = window_kv[:, 1].astype(jnp.float32)
        query_pos = index * TOK_DEV + jnp.arange(TOK_DEV, dtype=jnp.int32)
        key_pos = index * TOK_DEV - (WINDOW - 1) * TOK_DEV + jnp.arange(WINDOW * TOK_DEV, dtype=jnp.int32)
        allowed = (key_pos[None, :] >= 0) & (key_pos[None, :] <= query_pos[:, None])
        scores = jnp.einsum('thd,shd->hts', query.astype(jnp.float32), keys) / math.sqrt(HD)
        scores = jnp.where(allowed[None], scores, -jnp.inf)
        peak = lax.optimization_barrier(jnp.max(scores, axis=2, keepdims=True))
        expo = jnp.exp(scores - peak)
        total = lax.optimization_barrier(jnp.sum(expo, axis=2))
        rounded = lax.optimization_barrier(expo.astype(jnp.bfloat16)).astype(jnp.float32)
        output = jnp.einsum('hts,shd->thd', rounded, values) / total.T[:, :, None]
        return output.astype(jnp.bfloat16).reshape(TOK_DEV, head_cols)
    attended = lax.map(attend, (jnp.arange(N_CTX, dtype=jnp.int32), queries))
    return (mixer, attended.reshape(TOKENS, head_cols))
```

```python
from functools import reduce
import math

import jax
import jax.numpy as jnp
from jax import lax
from jax.sharding import PartitionSpec as P

HD = 128
TAPS = 7
WINDOW = 3
CHUNK = 128


EPSILON = 1e-06
PRECISE = lax.Precision.HIGHEST


def to_bf16_grid(value):
    return lax.reduce_precision(value, exponent_bits=8, mantissa_bits=7)


def from_behind(value, axis, steps):
    count = lax.axis_size(axis)
    leading, last = (max(0, -steps), min(count, count - steps))
    return lax.ppermute(value, axis, [(source, source + steps) for source in range(leading, last)])


def local_modal_conv(signal, decay, mixing):
    tokens, channels = signal.shape
    modes = decay.shape[0]
    chunks = tokens // CHUNK
    centre = (CHUNK - 1) / 2.0
    offsets = jnp.arange(CHUNK, dtype=jnp.float32) - centre
    up = jnp.exp(offsets[:, None, None] * decay[None])
    down = jnp.exp(-offsets[:, None, None] * decay[None])
    after = jnp.exp(-(jnp.arange(CHUNK, dtype=jnp.float32) + 1.0)[:, None, None] * decay[None])
    tri = (jnp.arange(CHUNK)[:, None] >= jnp.arange(CHUNK)[None, :]).astype(jnp.float32)
    blocks = signal.reshape(chunks, CHUNK, channels)
    lifted = (up[None] * blocks[:, :, None, :]).reshape(chunks, CHUNK, modes * channels)
    summed = jnp.einsum("ts,qsk->qtk", tri, lifted, precision=PRECISE).reshape(chunks, CHUNK, modes, channels)
    states = down[None] * summed
    intra = jnp.sum(states * mixing[None, None], axis=2)
    ends = states[:, CHUNK - 1]
    step = jnp.exp(-float(CHUNK) * decay)
    carry = jnp.zeros_like(decay)
    entering = []
    for chunk in range(chunks):
        entering.append(carry)
        carry = step * carry + ends[chunk]
    entering = jnp.stack(entering)
    weighted_after = after * mixing[None]
    return intra, entering, carry, weighted_after


def on_device(features, short_filter, decay_rate, residue, skip_gain, norm_gain, qkv_weight):
    tok_dev, _, channels = features.shape
    head_cols = qkv_weight.shape[2]
    shard_rows = lax.all_gather(qkv_weight, "ctx", axis=0, tiled=True)
    rim_rows = features[tok_dev - (TAPS - 1) :]
    before = from_behind(rim_rows, "ctx", 1)
    extended = jnp.concatenate([before, features], axis=0).astype(jnp.float32)
    short_conv = jnp.zeros((tok_dev, 3, channels), jnp.float32)
    for offset in range(TAPS):
        first_row = TAPS - 1 - offset
        short_conv = (
            short_conv
            + short_filter[:, offset, :][None] * extended[first_row : first_row + tok_dev]
        )
    gated = to_bf16_grid(short_conv[:, 1] * short_conv[:, 2])

    mixing = residue * jnp.sqrt(decay_rate)
    intra, entering, block_end, weighted_after = local_modal_conv(gated, decay_rate, mixing)

    block_step = jnp.exp(-float(tok_dev) * decay_rate)
    history = from_behind(block_end, "ctx", 1)
    factor = block_step
    count = lax.axis_size("ctx")
    shift = 1
    while shift < count:
        history = history + factor * from_behind(history, "ctx", shift)
        factor = factor * factor
        shift *= 2

    chunks = tok_dev // CHUNK
    chunk_step = jnp.exp(-float(CHUNK) * decay_rate)
    lead = [jnp.ones_like(decay_rate)]
    for chunk in range(1, chunks):
        lead.append(lead[-1] * chunk_step)
    lead = jnp.stack(lead)
    total_state = entering + lead * history[None]
    carried = jnp.einsum("lnc,qnc->qlc", weighted_after, total_state, precision=PRECISE)
    filtered = (intra + carried).reshape(tok_dev, channels) + skip_gain[None] * gated
    filtered = to_bf16_grid(filtered)
    mixer = (short_conv[:, 0] * filtered).astype(jnp.bfloat16)

    gathered = lax.all_gather(mixer, "tp", axis=1, tiled=True)
    as_float = gathered.astype(jnp.float32)
    inverse = lax.rsqrt(jnp.mean(as_float * as_float, axis=1, keepdims=True) + EPSILON)
    normed = (as_float * inverse * norm_gain[None]).astype(jnp.bfloat16)
    flat_rows = shard_rows.reshape(shard_rows.shape[0], 3 * head_cols)
    projected = jnp.dot(normed, flat_rows, preferred_element_type=jnp.float32).astype(jnp.bfloat16)
    heads = head_cols // HD
    query = projected[:, :head_cols].reshape(tok_dev, heads, HD)
    kv_pair = projected[:, head_cols:]
    blocks_kv = [kv_pair] + [from_behind(kv_pair, "ctx", lag) for lag in range(1, WINDOW)]
    position = lax.axis_index("ctx")
    row_ids = jnp.arange(tok_dev)
    causal = row_ids[:, None] >= row_ids[None, :]
    score_list = []
    for lag_step in range(WINDOW):
        keys = blocks_kv[lag_step][:, :head_cols].reshape(tok_dev, heads, HD)
        scores = jnp.einsum(
            "thd,shd->hts", query, keys, preferred_element_type=jnp.float32
        ) / math.sqrt(HD)
        if lag_step == 0:
            allowed = causal
        else:
            allowed = jnp.broadcast_to(position >= lag_step, causal.shape)
        score_list.append(jnp.where(allowed[None], scores, -jnp.inf))
    peak = reduce(jnp.maximum, [jnp.max(entry, axis=2) for entry in score_list])
    total = jnp.zeros((heads, tok_dev), jnp.float32)
    output = jnp.zeros((tok_dev, heads, HD), jnp.float32)
    for lag_step in range(WINDOW):
        expo = jnp.exp(score_list[lag_step] - peak[:, :, None])
        total = total + jnp.sum(expo, axis=2)
        values = blocks_kv[lag_step][:, head_cols:].reshape(tok_dev, heads, HD)
        output = output + jnp.einsum(
            "hts,shd->thd", expo.astype(jnp.bfloat16), values, preferred_element_type=jnp.float32
        )
    attended = (output / total.T[:, :, None]).astype(jnp.bfloat16).reshape(tok_dev, head_cols)
    return (mixer, attended)


def solution(mesh):
    placed = (
        P("ctx", None, "tp"),
        P(None, None, "tp"),
        P(None, "tp"),
        P(None, "tp"),
        P("tp"),
        P(),
        P("ctx", None, "tp"),
    )
    return jax.shard_map(
        on_device,
        mesh=mesh,
        in_specs=placed,
        out_specs=(P("ctx", "tp"), P("ctx", "tp")),
        check_vma=False,
    )
```

```python
from functools import reduce
import math

import jax
import jax.numpy as jnp
from jax import lax
from jax.sharding import PartitionSpec as P
from jax.experimental import pallas as pl
from jax.experimental.pallas import tpu as pltpu

HD = 128
TAPS = 7
WINDOW = 3
CHUNK = 128


EPSILON = 1e-06
PRECISE = lax.Precision.HIGHEST


def to_bf16_grid(value):
    return lax.reduce_precision(value, exponent_bits=8, mantissa_bits=7)


def from_behind(value, axis, steps):
    count = lax.axis_size(axis)
    leading, last = (max(0, -steps), min(count, count - steps))
    return lax.ppermute(value, axis, [(source, source + steps) for source in range(leading, last)])


def bf16_split(value):
    high = value.astype(jnp.bfloat16)
    low = (value - high.astype(jnp.float32)).astype(jnp.bfloat16)
    return high, low


def intra_kernel(gated_ref, decay_ref, mixing_ref, intra_ref, ends_ref):
    tokens, channels = gated_ref.shape
    chunks = tokens // CHUNK
    offsets = lax.broadcasted_iota(jnp.int32, (CHUNK, channels), 0).astype(jnp.float32) - (CHUNK - 1) / 2.0
    rows = lax.broadcasted_iota(jnp.int32, (CHUNK, CHUNK), 0)
    cols = lax.broadcasted_iota(jnp.int32, (CHUNK, CHUNK), 1)
    tri = (rows >= cols).astype(jnp.float32).astype(jnp.bfloat16)
    intra_ref[...] = jnp.zeros_like(intra_ref)

    def add_mode(mode, unused):
        rate = decay_ref[mode]
        weight = mixing_ref[mode]
        up = jnp.exp(offsets * rate)
        down = jnp.exp(-offsets * rate)
        for chunk in range(chunks):
            rows_of = pl.ds(chunk * CHUNK, CHUNK)
            high, low = bf16_split(up * gated_ref[rows_of, :])
            summed = jnp.dot(tri, high, preferred_element_type=jnp.float32) + jnp.dot(
                tri, low, preferred_element_type=jnp.float32
            )
            states = down * summed
            intra_ref[rows_of, :] += weight * states
            ends_ref[mode, pl.ds(chunk, 1), :] = states[CHUNK - 1 : CHUNK, :]
        return unused

    lax.fori_loop(0, decay_ref.shape[0], add_mode, 0)


def finish_kernel(intra_ref, state_ref, decay_ref, mixing_ref, gated_ref, first_ref, skip_ref, mixer_ref, acc_ref):
    tokens, channels = gated_ref.shape
    chunks = tokens // CHUNK
    after = lax.broadcasted_iota(jnp.int32, (CHUNK, channels), 0).astype(jnp.float32) + 1.0
    acc_ref[...] = intra_ref[...]

    def add_mode(mode, unused):
        decayed = jnp.exp(-after * decay_ref[mode]) * mixing_ref[mode]
        for chunk in range(chunks):
            rows_of = pl.ds(chunk * CHUNK, CHUNK)
            acc_ref[rows_of, :] += decayed * state_ref[mode, pl.ds(chunk, 1), :]
        return unused

    lax.fori_loop(0, decay_ref.shape[0], add_mode, 0)
    filtered = acc_ref[...] + skip_ref[...] * gated_ref[...]
    filtered = filtered.astype(jnp.bfloat16).astype(jnp.float32)
    mixer_ref[...] = (first_ref[...] * filtered).astype(mixer_ref.dtype)


def whole(shape, dtype):
    return jax.ShapeDtypeStruct(shape, dtype)


def in_vmem(count):
    return [pl.BlockSpec(memory_space=pltpu.VMEM)] * count


def intra_call(gated, decay3, mixing3):
    tokens, channels = gated.shape
    modes = decay3.shape[0]
    chunks = tokens // CHUNK
    return pl.pallas_call(
        intra_kernel,
        out_shape=(whole((tokens, channels), jnp.float32), whole((modes, chunks, channels), jnp.float32)),
        in_specs=in_vmem(3),
        out_specs=tuple(in_vmem(2)),
        cost_estimate=pl.CostEstimate(
            flops=4 * modes * tokens * CHUNK * channels, transcendentals=2 * modes * CHUNK * channels,
            bytes_accessed=8 * tokens * channels,
        ),
    )(gated, decay3, mixing3)


def finish_call(intra, entering, decay3, mixing3, gated, first, skip):
    tokens, channels = gated.shape
    modes = decay3.shape[0]
    return pl.pallas_call(
        finish_kernel,
        out_shape=whole((tokens, channels), jnp.bfloat16),
        in_specs=in_vmem(7),
        out_specs=pl.BlockSpec(memory_space=pltpu.VMEM),
        scratch_shapes=[pltpu.VMEM((tokens, channels), jnp.float32)],
        cost_estimate=pl.CostEstimate(
            flops=2 * modes * tokens * channels, transcendentals=modes * CHUNK * channels,
            bytes_accessed=14 * tokens * channels,
        ),
    )(intra, entering, decay3, mixing3, gated, first, skip)


def chunk_states(ends, decay):
    step = jnp.exp(-float(CHUNK) * decay)
    carry = jnp.zeros_like(decay)
    entering = []
    for chunk in range(ends.shape[1]):
        entering.append(carry)
        carry = step * carry + ends[:, chunk]
    return jnp.stack(entering, axis=1), carry


def on_device(features, short_filter, decay_rate, residue, skip_gain, norm_gain, qkv_weight):
    tok_dev, _, channels = features.shape
    head_cols = qkv_weight.shape[2]
    shard_rows = lax.all_gather(qkv_weight, "ctx", axis=0, tiled=True)
    rim_rows = features[tok_dev - (TAPS - 1) :]
    before = from_behind(rim_rows, "ctx", 1)
    extended = jnp.concatenate([before, features], axis=0).astype(jnp.float32)
    short_conv = jnp.zeros((tok_dev, 3, channels), jnp.float32)
    for offset in range(TAPS):
        first_row = TAPS - 1 - offset
        short_conv = (
            short_conv
            + short_filter[:, offset, :][None] * extended[first_row : first_row + tok_dev]
        )
    gated = to_bf16_grid(short_conv[:, 1] * short_conv[:, 2])

    mixing = residue * jnp.sqrt(decay_rate)
    decay3 = decay_rate[:, None, :]
    mixing3 = mixing[:, None, :]
    intra, ends = intra_call(gated, decay3, mixing3)
    entering, block_end = chunk_states(ends, decay_rate)

    count = lax.axis_size("ctx")
    history = jnp.zeros_like(decay_rate)
    for shift in range(1, count):
        arrived = from_behind(block_end, "ctx", shift)
        history = history + jnp.exp(-float((shift - 1) * tok_dev) * decay_rate) * arrived
    chunks = tok_dev // CHUNK
    lead = jnp.exp(-float(CHUNK) * jnp.arange(chunks, dtype=jnp.float32)[None, :, None] * decay_rate[:, None, :])
    total_state = entering + lead * history[:, None, :]
    mixer = finish_call(intra, total_state, decay3, mixing3, gated, short_conv[:, 0], skip_gain[None])

    parts = lax.axis_size("tp")
    me = lax.axis_index("tp")
    pieces = [mixer] + [
        lax.ppermute(mixer, "tp", [((source + shift) % parts, source) for source in range(parts)])
        for shift in range(1, parts)
    ]
    doubled = jnp.concatenate(pieces + pieces, axis=1)
    gathered = lax.dynamic_slice_in_dim(doubled, ((parts - me) % parts) * channels, parts * channels, 1)
    as_float = gathered.astype(jnp.float32)
    inverse = lax.rsqrt(jnp.mean(as_float * as_float, axis=1, keepdims=True) + EPSILON)
    normed = (as_float * inverse * norm_gain[None]).astype(jnp.bfloat16)
    flat_rows = shard_rows.reshape(shard_rows.shape[0], 3 * head_cols)
    projected = jnp.dot(normed, flat_rows, preferred_element_type=jnp.float32).astype(jnp.bfloat16)
    heads = head_cols // HD
    query = projected[:, :head_cols].reshape(tok_dev, heads, HD)
    kv_pair = projected[:, head_cols:]
    blocks_kv = [kv_pair] + [from_behind(kv_pair, "ctx", lag) for lag in range(1, WINDOW)]
    position = lax.axis_index("ctx")
    row_ids = jnp.arange(tok_dev)
    causal = row_ids[:, None] >= row_ids[None, :]
    score_list = []
    for lag_step in range(WINDOW):
        keys = blocks_kv[lag_step][:, :head_cols].reshape(tok_dev, heads, HD)
        scores = jnp.einsum(
            "thd,shd->hts", query, keys, preferred_element_type=jnp.float32
        ) / math.sqrt(HD)
        if lag_step == 0:
            allowed = causal
        else:
            allowed = jnp.broadcast_to(position >= lag_step, causal.shape)
        score_list.append(jnp.where(allowed[None], scores, -jnp.inf))
    peak = reduce(jnp.maximum, [jnp.max(entry, axis=2) for entry in score_list])
    total = jnp.zeros((heads, tok_dev), jnp.float32)
    output = jnp.zeros((tok_dev, heads, HD), jnp.float32)
    for lag_step in range(WINDOW):
        expo = jnp.exp(score_list[lag_step] - peak[:, :, None])
        total = total + jnp.sum(expo, axis=2)
        values = blocks_kv[lag_step][:, head_cols:].reshape(tok_dev, heads, HD)
        output = output + jnp.einsum(
            "hts,shd->thd", expo.astype(jnp.bfloat16), values, preferred_element_type=jnp.float32
        )
    attended = (output / total.T[:, :, None]).astype(jnp.bfloat16).reshape(tok_dev, head_cols)
    return (mixer, attended)


def solution(mesh):
    placed = (
        P("ctx", None, "tp"),
        P(None, None, "tp"),
        P(None, "tp"),
        P(None, "tp"),
        P("tp"),
        P(),
        P("ctx", None, "tp"),
    )
    return jax.shard_map(
        on_device,
        mesh=mesh,
        in_specs=placed,
        out_specs=(P("ctx", "tp"), P("ctx", "tp")),
        check_vma=False,
    )
```

```python
from functools import reduce
import math

import jax
import jax.numpy as jnp
from jax import lax
from jax.sharding import PartitionSpec as P
from jax.experimental import pallas as pl
from jax.experimental.pallas import tpu as pltpu

HD = 128
TAPS = 7
WINDOW = 3
CHUNK = 128
GROUP = 8


EPSILON = 1e-06
PRECISE = lax.Precision.HIGHEST


def to_bf16_grid(value):
    return lax.reduce_precision(value, exponent_bits=8, mantissa_bits=7)


def from_behind(value, axis, steps):
    count = lax.axis_size(axis)
    leading, last = (max(0, -steps), min(count, count - steps))
    return lax.ppermute(value, axis, [(source, source + steps) for source in range(leading, last)])


def bf16_split(value):
    high = value.astype(jnp.bfloat16)
    low = (value - high.astype(jnp.float32)).astype(jnp.bfloat16)
    return high, low


def intra_kernel(gated_ref, decay_ref, mixing_ref, intra_ref):
    tokens, channels = gated_ref.shape
    chunks = tokens // CHUNK
    offsets = lax.broadcasted_iota(jnp.int32, (CHUNK, channels), 0).astype(jnp.float32) - (CHUNK - 1) / 2.0
    rows = lax.broadcasted_iota(jnp.int32, (CHUNK, CHUNK), 0)
    cols = lax.broadcasted_iota(jnp.int32, (CHUNK, CHUNK), 1)
    tri = (rows >= cols).astype(jnp.float32).astype(jnp.bfloat16)
    intra_ref[...] = jnp.zeros_like(intra_ref)

    def add_mode(mode, unused):
        rate = decay_ref[mode]
        weight = mixing_ref[mode]
        up = jnp.exp(offsets * rate)
        down = jnp.exp(-offsets * rate)
        for chunk in range(chunks):
            rows_of = pl.ds(chunk * CHUNK, CHUNK)
            high, low = bf16_split(up * gated_ref[rows_of, :])
            summed = jnp.dot(tri, high, preferred_element_type=jnp.float32) + jnp.dot(
                tri, low, preferred_element_type=jnp.float32
            )
            states = down * summed
            intra_ref[rows_of, :] += weight * states
        return unused

    lax.fori_loop(0, decay_ref.shape[0], add_mode, 0)


def ends_kernel(gated_ref, decay_ref, ends_ref):
    tokens, channels = gated_ref.shape
    chunks = tokens // CHUNK
    tail = (CHUNK - 1) - lax.broadcasted_iota(jnp.int32, (CHUNK, channels), 0).astype(jnp.float32)

    def add_mode(mode, unused):
        fade = jnp.exp(-tail * decay_ref[mode])
        for chunk in range(chunks):
            block = gated_ref[pl.ds(chunk * CHUNK, CHUNK), :]
            ends_ref[mode, pl.ds(chunk, 1), :] = jnp.sum(fade * block, axis=0, keepdims=True)
        return unused

    lax.fori_loop(0, decay_ref.shape[0], add_mode, 0)


def finish_kernel(intra_ref, state_ref, decay_ref, mixing_ref, gated_ref, first_ref, skip_ref, mixer_ref, acc_ref):
    tokens, channels = gated_ref.shape
    chunks = tokens // CHUNK
    after = lax.broadcasted_iota(jnp.int32, (CHUNK, channels), 0).astype(jnp.float32) + 1.0
    acc_ref[...] = intra_ref[...]

    def add_mode(mode, unused):
        decayed = jnp.exp(-after * decay_ref[mode]) * mixing_ref[mode]
        for chunk in range(chunks):
            rows_of = pl.ds(chunk * CHUNK, CHUNK)
            acc_ref[rows_of, :] += decayed * state_ref[mode, pl.ds(chunk, 1), :]
        return unused

    lax.fori_loop(0, decay_ref.shape[0], add_mode, 0)
    filtered = acc_ref[...] + skip_ref[...] * gated_ref[...]
    filtered = filtered.astype(jnp.bfloat16).astype(jnp.float32)
    mixer_ref[...] = (first_ref[...] * filtered).astype(mixer_ref.dtype)


def whole(shape, dtype):
    return jax.ShapeDtypeStruct(shape, dtype)


def in_vmem(count):
    return [pl.BlockSpec(memory_space=pltpu.VMEM)] * count


def intra_call(gated, decay3, mixing3):
    tokens, channels = gated.shape
    modes = decay3.shape[0]
    chunks = tokens // CHUNK
    return pl.pallas_call(
        intra_kernel,
        out_shape=whole((tokens, channels), jnp.float32),
        in_specs=in_vmem(3),
        out_specs=pl.BlockSpec(memory_space=pltpu.VMEM),
        cost_estimate=pl.CostEstimate(
            flops=4 * modes * tokens * CHUNK * channels, transcendentals=2 * modes * CHUNK * channels,
            bytes_accessed=8 * tokens * channels,
        ),
    )(gated, decay3, mixing3)


def ends_call(gated, decay3):
    tokens, channels = gated.shape
    modes = decay3.shape[0]
    chunks = tokens // CHUNK
    return pl.pallas_call(
        ends_kernel,
        out_shape=whole((modes, chunks, channels), jnp.float32),
        in_specs=in_vmem(2),
        out_specs=pl.BlockSpec(memory_space=pltpu.VMEM),
        cost_estimate=pl.CostEstimate(
            flops=2 * modes * tokens * channels, transcendentals=modes * CHUNK * channels,
            bytes_accessed=4 * tokens * channels,
        ),
    )(gated, decay3)


def exchange_history(block_end, decay, tok_dev):
    count = lax.axis_size("ctx")
    group = math.gcd(count, GROUP)
    me = lax.axis_index("ctx")
    place = me % group

    def decayed(blocks):
        return jnp.exp(-(blocks.astype(jnp.float32) * float(tok_dev)) * decay)

    prefix = jnp.zeros_like(decay)
    total = decayed(group - 1 - place) * block_end
    for shift in range(1, group):
        pairs = [(g + q, g + (q + shift) % group) for g in range(0, count, group) for q in range(group)]
        arrived = lax.ppermute(block_end, "ctx", pairs)
        source = (place - shift) % group
        prefix = prefix + jnp.where(source < place, decayed(place - 1 - source), 0.0) * arrived
        total = total + decayed(group - 1 - source) * arrived
    entering = jnp.zeros_like(decay)
    for hop in range(1, count // group):
        arrived = from_behind(total, "ctx", hop * group)
        entering = entering + decayed(jnp.int32((hop - 1) * group)) * arrived
    return prefix + decayed(place) * entering


def finish_call(intra, entering, decay3, mixing3, gated, first, skip):
    tokens, channels = gated.shape
    modes = decay3.shape[0]
    return pl.pallas_call(
        finish_kernel,
        out_shape=whole((tokens, channels), jnp.bfloat16),
        in_specs=in_vmem(7),
        out_specs=pl.BlockSpec(memory_space=pltpu.VMEM),
        scratch_shapes=[pltpu.VMEM((tokens, channels), jnp.float32)],
        cost_estimate=pl.CostEstimate(
            flops=2 * modes * tokens * channels, transcendentals=modes * CHUNK * channels,
            bytes_accessed=14 * tokens * channels,
        ),
    )(intra, entering, decay3, mixing3, gated, first, skip)


def chunk_states(ends, decay):
    step = jnp.exp(-float(CHUNK) * decay)
    carry = jnp.zeros_like(decay)
    entering = []
    for chunk in range(ends.shape[1]):
        entering.append(carry)
        carry = step * carry + ends[:, chunk]
    return jnp.stack(entering, axis=1), carry


def on_device(features, short_filter, decay_rate, residue, skip_gain, norm_gain, qkv_weight):
    tok_dev, _, channels = features.shape
    head_cols = qkv_weight.shape[2]
    shard_rows = lax.all_gather(qkv_weight, "ctx", axis=0, tiled=True)
    rim_rows = features[tok_dev - (TAPS - 1) :]
    before = from_behind(rim_rows, "ctx", 1)
    extended = jnp.concatenate([before, features], axis=0).astype(jnp.float32)
    short_conv = jnp.zeros((tok_dev, 3, channels), jnp.float32)
    for offset in range(TAPS):
        first_row = TAPS - 1 - offset
        short_conv = (
            short_conv
            + short_filter[:, offset, :][None] * extended[first_row : first_row + tok_dev]
        )
    gated = to_bf16_grid(short_conv[:, 1] * short_conv[:, 2])

    mixing = residue * jnp.sqrt(decay_rate)
    decay3 = decay_rate[:, None, :]
    mixing3 = mixing[:, None, :]
    ends = ends_call(gated, decay3)
    entering, block_end = chunk_states(ends, decay_rate)
    history = exchange_history(block_end, decay_rate, tok_dev)
    intra = intra_call(gated, decay3, mixing3)
    chunks = tok_dev // CHUNK
    lead = jnp.exp(-float(CHUNK) * jnp.arange(chunks, dtype=jnp.float32)[None, :, None] * decay_rate[:, None, :])
    total_state = entering + lead * history[:, None, :]
    mixer = finish_call(intra, total_state, decay3, mixing3, gated, short_conv[:, 0], skip_gain[None])

    parts = lax.axis_size("tp")
    me = lax.axis_index("tp")
    pieces = [mixer] + [
        lax.ppermute(mixer, "tp", [((source + shift) % parts, source) for source in range(parts)])
        for shift in range(1, parts)
    ]
    doubled = jnp.concatenate(pieces + pieces, axis=1)
    gathered = lax.dynamic_slice_in_dim(doubled, ((parts - me) % parts) * channels, parts * channels, 1)
    as_float = gathered.astype(jnp.float32)
    inverse = lax.rsqrt(jnp.mean(as_float * as_float, axis=1, keepdims=True) + EPSILON)
    normed = (as_float * inverse * norm_gain[None]).astype(jnp.bfloat16)
    flat_rows = shard_rows.reshape(shard_rows.shape[0], 3 * head_cols)
    projected = jnp.dot(normed, flat_rows, preferred_element_type=jnp.float32).astype(jnp.bfloat16)
    heads = head_cols // HD
    query = projected[:, :head_cols].reshape(tok_dev, heads, HD)
    kv_pair = projected[:, head_cols:]
    blocks_kv = [kv_pair] + [from_behind(kv_pair, "ctx", lag) for lag in range(1, WINDOW)]
    position = lax.axis_index("ctx")
    row_ids = jnp.arange(tok_dev)
    causal = row_ids[:, None] >= row_ids[None, :]
    score_list = []
    for lag_step in range(WINDOW):
        keys = blocks_kv[lag_step][:, :head_cols].reshape(tok_dev, heads, HD)
        scores = jnp.einsum(
            "thd,shd->hts", query, keys, preferred_element_type=jnp.float32
        ) / math.sqrt(HD)
        if lag_step == 0:
            allowed = causal
        else:
            allowed = jnp.broadcast_to(position >= lag_step, causal.shape)
        score_list.append(jnp.where(allowed[None], scores, -jnp.inf))
    peak = reduce(jnp.maximum, [jnp.max(entry, axis=2) for entry in score_list])
    total = jnp.zeros((heads, tok_dev), jnp.float32)
    output = jnp.zeros((tok_dev, heads, HD), jnp.float32)
    for lag_step in range(WINDOW):
        expo = jnp.exp(score_list[lag_step] - peak[:, :, None])
        total = total + jnp.sum(expo, axis=2)
        values = blocks_kv[lag_step][:, head_cols:].reshape(tok_dev, heads, HD)
        output = output + jnp.einsum(
            "hts,shd->thd", expo.astype(jnp.bfloat16), values, preferred_element_type=jnp.float32
        )
    attended = (output / total.T[:, :, None]).astype(jnp.bfloat16).reshape(tok_dev, head_cols)
    return (mixer, attended)


def solution(mesh):
    placed = (
        P("ctx", None, "tp"),
        P(None, None, "tp"),
        P(None, "tp"),
        P(None, "tp"),
        P("tp"),
        P(),
        P("ctx", None, "tp"),
    )
    return jax.shard_map(
        on_device,
        mesh=mesh,
        in_specs=placed,
        out_specs=(P("ctx", "tp"), P("ctx", "tp")),
        check_vma=False,
    )
```

```python
from functools import reduce
import math

import jax
import jax.numpy as jnp
from jax import lax
from jax.sharding import PartitionSpec as P
from jax.experimental import pallas as pl
from jax.experimental.pallas import tpu as pltpu

HD = 128
TAPS = 7
WINDOW = 3
CHUNK = 128
GROUP = 8


EPSILON = 1e-06


def from_behind(value, axis, steps):
    count = lax.axis_size(axis)
    leading, last = (max(0, -steps), min(count, count - steps))
    return lax.ppermute(value, axis, [(source, source + steps) for source in range(leading, last)])


def bf16_split(value):
    high = value.astype(jnp.bfloat16)
    low = (value - high.astype(jnp.float32)).astype(jnp.bfloat16)
    return high, low


def intra_kernel(gated_ref, decay_ref, mixing_ref, intra_ref):
    tokens, channels = gated_ref.shape
    chunks = tokens // CHUNK
    offsets = lax.broadcasted_iota(jnp.int32, (CHUNK, channels), 0).astype(jnp.float32) - (CHUNK - 1) / 2.0
    rows = lax.broadcasted_iota(jnp.int32, (CHUNK, CHUNK), 0)
    cols = lax.broadcasted_iota(jnp.int32, (CHUNK, CHUNK), 1)
    tri = (rows >= cols).astype(jnp.float32).astype(jnp.bfloat16)
    intra_ref[...] = jnp.zeros_like(intra_ref)

    def add_mode(mode, unused):
        rate = decay_ref[mode]
        weight = mixing_ref[mode] * jnp.sqrt(rate)
        up = jnp.exp(offsets * rate)
        down = jnp.exp(-offsets * rate)
        for chunk in range(chunks):
            rows_of = pl.ds(chunk * CHUNK, CHUNK)
            high, low = bf16_split(up * gated_ref[rows_of, :])
            summed = jnp.dot(tri, high, preferred_element_type=jnp.float32) + jnp.dot(
                tri, low, preferred_element_type=jnp.float32
            )
            states = down * summed
            intra_ref[rows_of, :] += weight * states
        return unused

    lax.fori_loop(0, decay_ref.shape[0], add_mode, 0)


def front_kernel(feat_ref, halo_ref, taps_ref, decay_ref, first_ref, gated_ref, ends_ref, ext_ref):
    tokens, channels = first_ref.shape
    chunks = tokens // CHUNK
    lead = 8

    def short(stream, rows_of):
        taps = [taps_ref[stream, pl.ds(offset, 1), :] for offset in range(TAPS)]
        total = taps[0] * ext_ref[stream, pl.ds(lead + rows_of, CHUNK), :]
        for offset in range(1, TAPS):
            total = total + taps[offset] * ext_ref[stream, pl.ds(lead - offset + rows_of, CHUNK), :]
        return total

    for stream in range(3):
        cols = pl.ds(stream * channels, channels)
        ext_ref[stream, pl.ds(lead - (TAPS - 1), TAPS - 1), :] = halo_ref[:, cols].astype(jnp.float32)
        ext_ref[stream, pl.ds(lead, tokens), :] = feat_ref[:, cols].astype(jnp.float32)
    for chunk in range(chunks):
        rows_of = chunk * CHUNK
        first_ref[pl.ds(rows_of, CHUNK), :] = short(0, rows_of)
        product = short(1, rows_of) * short(2, rows_of)
        gated_ref[pl.ds(rows_of, CHUNK), :] = product.astype(jnp.bfloat16).astype(jnp.float32)

    tail = (CHUNK - 1) - lax.broadcasted_iota(jnp.int32, (CHUNK, channels), 0).astype(jnp.float32)

    def add_mode(mode, unused):
        fade = jnp.exp(-tail * decay_ref[mode])
        for chunk in range(chunks):
            block = gated_ref[pl.ds(chunk * CHUNK, CHUNK), :]
            ends_ref[mode, pl.ds(chunk, 1), :] = jnp.sum(fade * block, axis=0, keepdims=True)
        return unused

    lax.fori_loop(0, decay_ref.shape[0], add_mode, 0)


def front_call(features, halo, short_filter, decay3):
    tokens, streams, channels = features.shape
    modes = decay3.shape[0]
    chunks = tokens // CHUNK
    return pl.pallas_call(
        front_kernel,
        out_shape=(
            whole((tokens, channels), jnp.float32),
            whole((tokens, channels), jnp.float32),
            whole((modes, chunks, channels), jnp.float32),
        ),
        in_specs=in_vmem(4),
        out_specs=tuple(in_vmem(3)),
        scratch_shapes=[pltpu.VMEM((streams, tokens + 8, channels), jnp.float32)],
        cost_estimate=pl.CostEstimate(
            flops=2 * (3 * TAPS + modes) * tokens * channels, transcendentals=modes * CHUNK * channels,
            bytes_accessed=14 * tokens * channels,
        ),
    )(features.reshape(tokens, streams * channels), halo.reshape(halo.shape[0], streams * channels), short_filter, decay3)


def finish_kernel(intra_ref, state_ref, decay_ref, mixing_ref, gated_ref, first_ref, skip_ref, mixer_ref, acc_ref):
    tokens, channels = gated_ref.shape
    chunks = tokens // CHUNK
    after = lax.broadcasted_iota(jnp.int32, (CHUNK, channels), 0).astype(jnp.float32) + 1.0
    acc_ref[...] = intra_ref[...]

    def add_mode(mode, unused):
        rate = decay_ref[mode]
        decayed = jnp.exp(-after * rate) * (mixing_ref[mode] * jnp.sqrt(rate))
        for chunk in range(chunks):
            rows_of = pl.ds(chunk * CHUNK, CHUNK)
            acc_ref[rows_of, :] += decayed * state_ref[mode, pl.ds(chunk, 1), :]
        return unused

    lax.fori_loop(0, decay_ref.shape[0], add_mode, 0)
    filtered = acc_ref[...] + skip_ref[...] * gated_ref[...]
    filtered = filtered.astype(jnp.bfloat16).astype(jnp.float32)
    mixer_ref[...] = (first_ref[...] * filtered).astype(mixer_ref.dtype)


def whole(shape, dtype):
    return jax.ShapeDtypeStruct(shape, dtype)


def in_vmem(count):
    return [pl.BlockSpec(memory_space=pltpu.VMEM)] * count


def intra_call(gated, decay3, mixing3):
    tokens, channels = gated.shape
    modes = decay3.shape[0]
    return pl.pallas_call(
        intra_kernel,
        out_shape=whole((tokens, channels), jnp.float32),
        in_specs=in_vmem(3),
        out_specs=pl.BlockSpec(memory_space=pltpu.VMEM),
        cost_estimate=pl.CostEstimate(
            flops=4 * modes * tokens * CHUNK * channels, transcendentals=2 * modes * CHUNK * channels,
            bytes_accessed=8 * tokens * channels,
        ),
    )(gated, decay3, mixing3)


def exchange_history(block_end, decay, tok_dev):
    count = lax.axis_size("ctx")
    group = math.gcd(count, GROUP)
    me = lax.axis_index("ctx")
    place = me % group

    def decayed(blocks):
        return jnp.exp(-(blocks.astype(jnp.float32) * float(tok_dev)) * decay)

    prefix = jnp.zeros_like(decay)
    total = decayed(group - 1 - place) * block_end
    for shift in range(1, group):
        pairs = [(g + q, g + (q + shift) % group) for g in range(0, count, group) for q in range(group)]
        arrived = lax.ppermute(block_end, "ctx", pairs)
        source = (place - shift) % group
        prefix = prefix + jnp.where(source < place, decayed(place - 1 - source), 0.0) * arrived
        total = total + decayed(group - 1 - source) * arrived
    entering = jnp.zeros_like(decay)
    for hop in range(1, count // group):
        arrived = from_behind(total, "ctx", hop * group)
        entering = entering + decayed(jnp.int32((hop - 1) * group)) * arrived
    return prefix + decayed(place) * entering


def finish_call(intra, entering, decay3, mixing3, gated, first, skip):
    tokens, channels = gated.shape
    modes = decay3.shape[0]
    return pl.pallas_call(
        finish_kernel,
        out_shape=whole((tokens, channels), jnp.bfloat16),
        in_specs=in_vmem(7),
        out_specs=pl.BlockSpec(memory_space=pltpu.VMEM),
        scratch_shapes=[pltpu.VMEM((tokens, channels), jnp.float32)],
        cost_estimate=pl.CostEstimate(
            flops=2 * modes * tokens * channels, transcendentals=modes * CHUNK * channels,
            bytes_accessed=14 * tokens * channels,
        ),
    )(intra, entering, decay3, mixing3, gated, first, skip)


def chunk_states(ends, decay):
    step = jnp.exp(-float(CHUNK) * decay)
    carry = jnp.zeros_like(decay)
    entering = []
    for chunk in range(ends.shape[1]):
        entering.append(carry)
        carry = step * carry + ends[:, chunk]
    return jnp.stack(entering, axis=1), carry


def block_body(features, short_filter, decay_rate, residue, skip_gain, norm_gain, qkv_weight):
    tok_dev, _, channels = features.shape
    head_cols = qkv_weight.shape[2]
    shard_rows = lax.all_gather(qkv_weight, "ctx", axis=0, tiled=True)
    rim_rows = features[tok_dev - (TAPS - 1) :]
    before = from_behind(rim_rows, "ctx", 1)
    decay3 = decay_rate[:, None, :]
    mixing3 = residue[:, None, :]
    first, gated, ends = front_call(features, before, short_filter, decay3)
    entering, block_end = chunk_states(ends, decay_rate)
    history = exchange_history(block_end, decay_rate, tok_dev)
    intra = intra_call(gated, decay3, mixing3)
    chunks = tok_dev // CHUNK
    lead = jnp.exp(-float(CHUNK) * jnp.arange(chunks, dtype=jnp.float32)[None, :, None] * decay_rate[:, None, :])
    total_state = entering + lead * history[:, None, :]
    mixer = finish_call(intra, total_state, decay3, mixing3, gated, first, skip_gain[None])

    parts = lax.axis_size("tp")
    me = lax.axis_index("tp")
    pieces = [mixer] + [
        lax.ppermute(mixer, "tp", [((source + shift) % parts, source) for source in range(parts)])
        for shift in range(1, parts)
    ]
    doubled = jnp.concatenate(pieces + pieces, axis=1)
    gathered = lax.dynamic_slice_in_dim(doubled, ((parts - me) % parts) * channels, parts * channels, 1)
    as_float = gathered.astype(jnp.float32)
    inverse = lax.rsqrt(jnp.mean(as_float * as_float, axis=1, keepdims=True) + EPSILON)
    normed = (as_float * inverse * norm_gain[None]).astype(jnp.bfloat16)
    flat_rows = shard_rows.reshape(shard_rows.shape[0], 3 * head_cols)
    projected = jnp.dot(normed, flat_rows, preferred_element_type=jnp.float32).astype(jnp.bfloat16)
    heads = head_cols // HD
    query = projected[:, :head_cols].reshape(tok_dev, heads, HD)
    kv_pair = projected[:, head_cols:]
    blocks_kv = [kv_pair]
    for _ in range(WINDOW - 1):
        blocks_kv.append(from_behind(blocks_kv[-1], "ctx", 1))
    position = lax.axis_index("ctx")
    row_ids = jnp.arange(tok_dev)
    causal = row_ids[:, None] >= row_ids[None, :]
    score_list = []
    for lag_step in range(WINDOW):
        keys = blocks_kv[lag_step][:, :head_cols].reshape(tok_dev, heads, HD)
        scores = jnp.einsum(
            "thd,shd->hts", query, keys, preferred_element_type=jnp.float32
        ) / math.sqrt(HD)
        if lag_step == 0:
            allowed = causal
        else:
            allowed = jnp.broadcast_to(position >= lag_step, causal.shape)
        score_list.append(jnp.where(allowed[None], scores, -jnp.inf))
    peak = reduce(jnp.maximum, [jnp.max(entry, axis=2) for entry in score_list])
    total = jnp.zeros((heads, tok_dev), jnp.float32)
    output = jnp.zeros((tok_dev, heads, HD), jnp.float32)
    for lag_step in range(WINDOW):
        expo = jnp.exp(score_list[lag_step] - peak[:, :, None])
        total = total + jnp.sum(expo, axis=2)
        values = blocks_kv[lag_step][:, head_cols:].reshape(tok_dev, heads, HD)
        output = output + jnp.einsum(
            "hts,shd->thd", expo.astype(jnp.bfloat16), values, preferred_element_type=jnp.float32
        )
    attended = (output / total.T[:, :, None]).astype(jnp.bfloat16).reshape(tok_dev, head_cols)
    return (mixer, attended)


def solution(mesh):
    placed = (
        P("ctx", None, "tp"),
        P(None, None, "tp"),
        P(None, "tp"),
        P(None, "tp"),
        P("tp"),
        P(),
        P("ctx", None, "tp"),
    )
    return jax.shard_map(
        block_body,
        mesh=mesh,
        in_specs=placed,
        out_specs=(P("ctx", "tp"), P("ctx", "tp")),
        check_vma=False,
    )
```

```python
from functools import reduce
import math

import jax
import jax.numpy as jnp
from jax import lax
from jax.sharding import PartitionSpec as P
from jax.experimental import pallas as pl
from jax.experimental.pallas import tpu as pltpu

HD = 128
TAPS = 7
WINDOW = 3
CHUNK = 128
GROUP = 8


EPSILON = 1e-06


def from_behind(value, axis, steps):
    count = lax.axis_size(axis)
    leading, last = (max(0, -steps), min(count, count - steps))
    return lax.ppermute(value, axis, [(source, source + steps) for source in range(leading, last)])


def bf16_split(value):
    high = value.astype(jnp.bfloat16)
    low = (value - high.astype(jnp.float32)).astype(jnp.bfloat16)
    return high, low


def intra_kernel(gated_ref, decay_ref, mixing_ref, intra_ref):
    tokens, channels = gated_ref.shape
    chunks = tokens // CHUNK
    offsets = lax.broadcasted_iota(jnp.int32, (CHUNK, channels), 0).astype(jnp.float32) - (CHUNK - 1) / 2.0
    rows = lax.broadcasted_iota(jnp.int32, (CHUNK, CHUNK), 0)
    cols = lax.broadcasted_iota(jnp.int32, (CHUNK, CHUNK), 1)
    tri = (rows >= cols).astype(jnp.float32).astype(jnp.bfloat16)
    intra_ref[...] = jnp.zeros_like(intra_ref)

    def add_mode(mode, unused):
        rate = decay_ref[mode]
        weight = mixing_ref[mode] * jnp.sqrt(rate)
        up = jnp.exp(offsets * rate)
        down = jnp.exp(-offsets * rate)
        for chunk in range(chunks):
            rows_of = pl.ds(chunk * CHUNK, CHUNK)
            high, low = bf16_split(up * gated_ref[rows_of, :])
            summed = jnp.dot(tri, high, preferred_element_type=jnp.float32) + jnp.dot(
                tri, low, preferred_element_type=jnp.float32
            )
            states = down * summed
            intra_ref[rows_of, :] += weight * states
        return unused

    lax.fori_loop(0, decay_ref.shape[0], add_mode, 0)


def front_kernel(feat_ref, halo_ref, taps_ref, decay_ref, first_ref, gated_ref, ends_ref, ext_ref):
    tokens, channels = first_ref.shape
    chunks = tokens // CHUNK
    lead = 8

    def short(stream, rows_of):
        taps = [taps_ref[stream, pl.ds(offset, 1), :] for offset in range(TAPS)]
        total = taps[0] * ext_ref[stream, pl.ds(lead + rows_of, CHUNK), :]
        for offset in range(1, TAPS):
            total = total + taps[offset] * ext_ref[stream, pl.ds(lead - offset + rows_of, CHUNK), :]
        return total

    for stream in range(3):
        cols = pl.ds(stream * channels, channels)
        ext_ref[stream, pl.ds(lead - (TAPS - 1), TAPS - 1), :] = halo_ref[:, cols].astype(jnp.float32)
        ext_ref[stream, pl.ds(lead, tokens), :] = feat_ref[:, cols].astype(jnp.float32)
    for chunk in range(chunks):
        rows_of = chunk * CHUNK
        first_ref[pl.ds(rows_of, CHUNK), :] = short(0, rows_of)
        product = short(1, rows_of) * short(2, rows_of)
        gated_ref[pl.ds(rows_of, CHUNK), :] = product.astype(jnp.bfloat16).astype(jnp.float32)

    tail = (CHUNK - 1) - lax.broadcasted_iota(jnp.int32, (CHUNK, channels), 0).astype(jnp.float32)

    def add_mode(mode, unused):
        fade = jnp.exp(-tail * decay_ref[mode])
        for chunk in range(chunks):
            block = gated_ref[pl.ds(chunk * CHUNK, CHUNK), :]
            ends_ref[mode, pl.ds(chunk, 1), :] = jnp.sum(fade * block, axis=0, keepdims=True)
        return unused

    lax.fori_loop(0, decay_ref.shape[0], add_mode, 0)


def front_call(features, halo, short_filter, decay3):
    tokens, streams, channels = features.shape
    modes = decay3.shape[0]
    chunks = tokens // CHUNK
    return pl.pallas_call(
        front_kernel,
        out_shape=(
            whole((tokens, channels), jnp.float32),
            whole((tokens, channels), jnp.float32),
            whole((modes, chunks, channels), jnp.float32),
        ),
        in_specs=in_vmem(4),
        out_specs=tuple(in_vmem(3)),
        scratch_shapes=[pltpu.VMEM((streams, tokens + 8, channels), jnp.float32)],
        cost_estimate=pl.CostEstimate(
            flops=2 * (3 * TAPS + modes) * tokens * channels, transcendentals=modes * CHUNK * channels,
            bytes_accessed=14 * tokens * channels,
        ),
    )(features.reshape(tokens, streams * channels), halo.reshape(halo.shape[0], streams * channels), short_filter, decay3)


def finish_kernel(intra_ref, state_ref, decay_ref, mixing_ref, gated_ref, first_ref, skip_ref, mixer_ref, acc_ref):
    tokens, channels = gated_ref.shape
    chunks = tokens // CHUNK
    after = lax.broadcasted_iota(jnp.int32, (CHUNK, channels), 0).astype(jnp.float32) + 1.0
    acc_ref[...] = intra_ref[...]

    def add_mode(mode, unused):
        rate = decay_ref[mode]
        decayed = jnp.exp(-after * rate) * (mixing_ref[mode] * jnp.sqrt(rate))
        for chunk in range(chunks):
            rows_of = pl.ds(chunk * CHUNK, CHUNK)
            acc_ref[rows_of, :] += decayed * state_ref[mode, pl.ds(chunk, 1), :]
        return unused

    lax.fori_loop(0, decay_ref.shape[0], add_mode, 0)
    filtered = acc_ref[...] + skip_ref[...] * gated_ref[...]
    filtered = filtered.astype(jnp.bfloat16).astype(jnp.float32)
    mixer_ref[...] = (first_ref[...] * filtered).astype(mixer_ref.dtype)


def whole(shape, dtype):
    return jax.ShapeDtypeStruct(shape, dtype)


def in_vmem(count):
    return [pl.BlockSpec(memory_space=pltpu.VMEM)] * count


def intra_call(gated, decay3, mixing3):
    tokens, channels = gated.shape
    modes = decay3.shape[0]
    return pl.pallas_call(
        intra_kernel,
        out_shape=whole((tokens, channels), jnp.float32),
        in_specs=in_vmem(3),
        out_specs=pl.BlockSpec(memory_space=pltpu.VMEM),
        cost_estimate=pl.CostEstimate(
            flops=4 * modes * tokens * CHUNK * channels, transcendentals=2 * modes * CHUNK * channels,
            bytes_accessed=8 * tokens * channels,
        ),
    )(gated, decay3, mixing3)


def exchange_history(block_end, decay, tok_dev):
    count = lax.axis_size("ctx")
    group = math.gcd(count, GROUP)
    me = lax.axis_index("ctx")
    place = me % group

    def decayed(blocks):
        return jnp.exp(-(blocks.astype(jnp.float32) * float(tok_dev)) * decay)

    prefix = jnp.zeros_like(decay)
    total = decayed(group - 1 - place) * block_end
    for shift in range(1, group):
        pairs = [(g + q, g + (q + shift) % group) for g in range(0, count, group) for q in range(group)]
        arrived = lax.ppermute(block_end, "ctx", pairs)
        source = (place - shift) % group
        prefix = prefix + jnp.where(source < place, decayed(place - 1 - source), 0.0) * arrived
        total = total + decayed(group - 1 - source) * arrived
    entering = jnp.zeros_like(decay)
    for hop in range(1, count // group):
        arrived = from_behind(total, "ctx", hop * group)
        entering = entering + decayed(jnp.int32((hop - 1) * group)) * arrived
    return prefix + decayed(place) * entering


def finish_call(intra, entering, decay3, mixing3, gated, first, skip):
    tokens, channels = gated.shape
    modes = decay3.shape[0]
    return pl.pallas_call(
        finish_kernel,
        out_shape=whole((tokens, channels), jnp.bfloat16),
        in_specs=in_vmem(7),
        out_specs=pl.BlockSpec(memory_space=pltpu.VMEM),
        scratch_shapes=[pltpu.VMEM((tokens, channels), jnp.float32)],
        cost_estimate=pl.CostEstimate(
            flops=2 * modes * tokens * channels, transcendentals=modes * CHUNK * channels,
            bytes_accessed=14 * tokens * channels,
        ),
    )(intra, entering, decay3, mixing3, gated, first, skip)


def chunk_states(ends, decay):
    step = jnp.exp(-float(CHUNK) * decay)
    carry = jnp.zeros_like(decay)
    entering = []
    for chunk in range(ends.shape[1]):
        entering.append(carry)
        carry = step * carry + ends[:, chunk]
    return jnp.stack(entering, axis=1), carry


def gather_channels(block):
    parts = lax.axis_size("tp")
    me = lax.axis_index("tp")
    channels = block.shape[1]
    partner = lax.ppermute(block, "tp", [(source, source ^ 1) for source in range(parts)])
    low = me % 2 == 0
    pair = jnp.where(low, jnp.concatenate([block, partner], axis=1), jnp.concatenate([partner, block], axis=1))
    rings = parts // 2
    pieces = [pair] + [
        lax.ppermute(pair, "tp", [(source, (source + 2 * shift) % parts) for source in range(parts)])
        for shift in range(1, rings)
    ]
    ordered = [pieces[(-place) % rings] for place in range(rings)]
    doubled = jnp.concatenate(ordered + ordered, axis=1)
    first_pair = ((rings - me // 2) % rings) * 2 * channels
    return lax.dynamic_slice_in_dim(doubled, first_pair, parts * channels, 1)


def block_body(features, short_filter, decay_rate, residue, skip_gain, norm_gain, qkv_weight):
    tok_dev, _, _ = features.shape
    head_cols = qkv_weight.shape[2]
    shard_rows = lax.all_gather(qkv_weight, "ctx", axis=0, tiled=True)
    rim_rows = features[tok_dev - (TAPS - 1) :]
    before = from_behind(rim_rows, "ctx", 1)
    decay3 = decay_rate[:, None, :]
    mixing3 = residue[:, None, :]
    first, gated, ends = front_call(features, before, short_filter, decay3)
    entering, block_end = chunk_states(ends, decay_rate)
    history = exchange_history(block_end, decay_rate, tok_dev)
    intra = intra_call(gated, decay3, mixing3)
    chunks = tok_dev // CHUNK
    lead = jnp.exp(-float(CHUNK) * jnp.arange(chunks, dtype=jnp.float32)[None, :, None] * decay_rate[:, None, :])
    total_state = entering + lead * history[:, None, :]
    mixer = finish_call(intra, total_state, decay3, mixing3, gated, first, skip_gain[None])

    gathered = gather_channels(mixer)
    as_float = gathered.astype(jnp.float32)
    inverse = lax.rsqrt(jnp.mean(as_float * as_float, axis=1, keepdims=True) + EPSILON)
    normed = (as_float * inverse * norm_gain[None]).astype(jnp.bfloat16)
    flat_rows = shard_rows.reshape(shard_rows.shape[0], 3 * head_cols)
    projected = jnp.dot(normed, flat_rows, preferred_element_type=jnp.float32).astype(jnp.bfloat16)
    heads = head_cols // HD
    query = projected[:, :head_cols].reshape(tok_dev, heads, HD)
    kv_pair = projected[:, head_cols:]
    blocks_kv = [kv_pair]
    for _ in range(WINDOW - 1):
        blocks_kv.append(from_behind(blocks_kv[-1], "ctx", 1))
    position = lax.axis_index("ctx")
    row_ids = jnp.arange(tok_dev)
    causal = row_ids[:, None] >= row_ids[None, :]
    score_list = []
    for lag_step in range(WINDOW):
        keys = blocks_kv[lag_step][:, :head_cols].reshape(tok_dev, heads, HD)
        scores = jnp.einsum(
            "thd,shd->hts", query, keys, preferred_element_type=jnp.float32
        ) / math.sqrt(HD)
        if lag_step == 0:
            allowed = causal
        else:
            allowed = jnp.broadcast_to(position >= lag_step, causal.shape)
        score_list.append(jnp.where(allowed[None], scores, -jnp.inf))
    peak = reduce(jnp.maximum, [jnp.max(entry, axis=2) for entry in score_list])
    total = jnp.zeros((heads, tok_dev), jnp.float32)
    output = jnp.zeros((tok_dev, heads, HD), jnp.float32)
    for lag_step in range(WINDOW):
        expo = jnp.exp(score_list[lag_step] - peak[:, :, None])
        total = total + jnp.sum(expo, axis=2)
        values = blocks_kv[lag_step][:, head_cols:].reshape(tok_dev, heads, HD)
        output = output + jnp.einsum(
            "hts,shd->thd", expo.astype(jnp.bfloat16), values, preferred_element_type=jnp.float32
        )
    attended = (output / total.T[:, :, None]).astype(jnp.bfloat16).reshape(tok_dev, head_cols)
    return (mixer, attended)


def solution(mesh):
    placed = (
        P("ctx", None, "tp"),
        P(None, None, "tp"),
        P(None, "tp"),
        P(None, "tp"),
        P("tp"),
        P(),
        P("ctx", None, "tp"),
    )
    return jax.shard_map(
        block_body,
        mesh=mesh,
        in_specs=placed,
        out_specs=(P("ctx", "tp"), P("ctx", "tp")),
        check_vma=False,
    )
```

```python
from functools import reduce
import math

import jax
import jax.numpy as jnp
from jax import lax
from jax.sharding import PartitionSpec as P
from jax.experimental import pallas as pl
from jax.experimental.pallas import tpu as pltpu

HD = 128
TAPS = 7
WINDOW = 3
CHUNK = 128
GROUP = 8


EPSILON = 1e-06


def from_behind(value, axis, steps):
    count = lax.axis_size(axis)
    leading, last = (max(0, -steps), min(count, count - steps))
    return lax.ppermute(value, axis, [(source, source + steps) for source in range(leading, last)])


def bf16_split(value):
    high = value.astype(jnp.bfloat16)
    low = (value - high.astype(jnp.float32)).astype(jnp.bfloat16)
    return high, low


def intra_kernel(gated_ref, decay_ref, mixing_ref, intra_ref):
    tokens, channels = gated_ref.shape
    chunks = tokens // CHUNK
    offsets = lax.broadcasted_iota(jnp.int32, (CHUNK, channels), 0).astype(jnp.float32) - (CHUNK - 1) / 2.0
    rows = lax.broadcasted_iota(jnp.int32, (CHUNK, CHUNK), 0)
    cols = lax.broadcasted_iota(jnp.int32, (CHUNK, CHUNK), 1)
    tri = (rows >= cols).astype(jnp.float32).astype(jnp.bfloat16)
    intra_ref[...] = jnp.zeros_like(intra_ref)

    def add_mode(mode, unused):
        rate = decay_ref[mode]
        weight = mixing_ref[mode] * jnp.sqrt(rate)
        up = jnp.exp(offsets * rate)
        down = jnp.exp(-offsets * rate)
        for chunk in range(chunks):
            rows_of = pl.ds(chunk * CHUNK, CHUNK)
            high, low = bf16_split(up * gated_ref[rows_of, :])
            summed = jnp.dot(tri, high, preferred_element_type=jnp.float32) + jnp.dot(
                tri, low, preferred_element_type=jnp.float32
            )
            states = down * summed
            intra_ref[rows_of, :] += weight * states
        return unused

    lax.fori_loop(0, decay_ref.shape[0], add_mode, 0)


def front_kernel(feat_ref, halo_ref, taps_ref, decay_ref, first_ref, gated_ref, ends_ref, ext_ref):
    tokens, channels = first_ref.shape
    chunks = tokens // CHUNK
    lead = 8

    def short(stream, rows_of):
        taps = [taps_ref[stream, pl.ds(offset, 1), :] for offset in range(TAPS)]
        total = taps[0] * ext_ref[stream, pl.ds(lead + rows_of, CHUNK), :]
        for offset in range(1, TAPS):
            total = total + taps[offset] * ext_ref[stream, pl.ds(lead - offset + rows_of, CHUNK), :]
        return total

    for stream in range(3):
        cols = pl.ds(stream * channels, channels)
        ext_ref[stream, pl.ds(lead - (TAPS - 1), TAPS - 1), :] = halo_ref[:, cols].astype(jnp.float32)
        ext_ref[stream, pl.ds(lead, tokens), :] = feat_ref[:, cols].astype(jnp.float32)
    for chunk in range(chunks):
        rows_of = chunk * CHUNK
        first_ref[pl.ds(rows_of, CHUNK), :] = short(0, rows_of)
        product = short(1, rows_of) * short(2, rows_of)
        gated_ref[pl.ds(rows_of, CHUNK), :] = product.astype(jnp.bfloat16).astype(jnp.float32)

    tail = (CHUNK - 1) - lax.broadcasted_iota(jnp.int32, (CHUNK, channels), 0).astype(jnp.float32)

    def add_mode(mode, unused):
        fade = jnp.exp(-tail * decay_ref[mode])
        for chunk in range(chunks):
            block = gated_ref[pl.ds(chunk * CHUNK, CHUNK), :]
            ends_ref[mode, pl.ds(chunk, 1), :] = jnp.sum(fade * block, axis=0, keepdims=True)
        return unused

    lax.fori_loop(0, decay_ref.shape[0], add_mode, 0)


def front_call(features, halo, short_filter, decay3):
    tokens, streams, channels = features.shape
    modes = decay3.shape[0]
    chunks = tokens // CHUNK
    return pl.pallas_call(
        front_kernel,
        out_shape=(
            whole((tokens, channels), jnp.float32),
            whole((tokens, channels), jnp.float32),
            whole((modes, chunks, channels), jnp.float32),
        ),
        in_specs=in_vmem(4),
        out_specs=tuple(in_vmem(3)),
        scratch_shapes=[pltpu.VMEM((streams, tokens + 8, channels), jnp.float32)],
        cost_estimate=pl.CostEstimate(
            flops=2 * (3 * TAPS + modes) * tokens * channels, transcendentals=modes * CHUNK * channels,
            bytes_accessed=14 * tokens * channels,
        ),
    )(features.reshape(tokens, streams * channels), halo.reshape(halo.shape[0], streams * channels), short_filter, decay3)


def finish_kernel(intra_ref, state_ref, decay_ref, mixing_ref, gated_ref, first_ref, skip_ref, mixer_ref, acc_ref):
    tokens, channels = gated_ref.shape
    chunks = tokens // CHUNK
    after = lax.broadcasted_iota(jnp.int32, (CHUNK, channels), 0).astype(jnp.float32) + 1.0
    acc_ref[...] = intra_ref[...]

    def add_mode(mode, unused):
        rate = decay_ref[mode]
        decayed = jnp.exp(-after * rate) * (mixing_ref[mode] * jnp.sqrt(rate))
        for chunk in range(chunks):
            rows_of = pl.ds(chunk * CHUNK, CHUNK)
            acc_ref[rows_of, :] += decayed * state_ref[mode, pl.ds(chunk, 1), :]
        return unused

    lax.fori_loop(0, decay_ref.shape[0], add_mode, 0)
    filtered = acc_ref[...] + skip_ref[...] * gated_ref[...]
    filtered = filtered.astype(jnp.bfloat16).astype(jnp.float32)
    mixer_ref[...] = (first_ref[...] * filtered).astype(mixer_ref.dtype)


def whole(shape, dtype):
    return jax.ShapeDtypeStruct(shape, dtype)


def in_vmem(count):
    return [pl.BlockSpec(memory_space=pltpu.VMEM)] * count


def intra_call(gated, decay3, mixing3):
    tokens, channels = gated.shape
    modes = decay3.shape[0]
    return pl.pallas_call(
        intra_kernel,
        out_shape=whole((tokens, channels), jnp.float32),
        in_specs=in_vmem(3),
        out_specs=pl.BlockSpec(memory_space=pltpu.VMEM),
        cost_estimate=pl.CostEstimate(
            flops=4 * modes * tokens * CHUNK * channels, transcendentals=2 * modes * CHUNK * channels,
            bytes_accessed=8 * tokens * channels,
        ),
    )(gated, decay3, mixing3)


def exchange_history(block_end, decay, tok_dev):
    count = lax.axis_size("ctx")
    group = math.gcd(count, GROUP)
    me = lax.axis_index("ctx")
    place = me % group

    def decayed(blocks):
        return jnp.exp(-(blocks.astype(jnp.float32) * float(tok_dev)) * decay)

    prefix = jnp.zeros_like(decay)
    total = decayed(group - 1 - place) * block_end
    for shift in range(1, group):
        pairs = [(g + q, g + (q + shift) % group) for g in range(0, count, group) for q in range(group)]
        arrived = lax.ppermute(block_end, "ctx", pairs)
        source = (place - shift) % group
        prefix = prefix + jnp.where(source < place, decayed(place - 1 - source), 0.0) * arrived
        total = total + decayed(group - 1 - source) * arrived
    entering = jnp.zeros_like(decay)
    for hop in range(1, count // group):
        arrived = from_behind(total, "ctx", hop * group)
        entering = entering + decayed(jnp.int32((hop - 1) * group)) * arrived
    return prefix + decayed(place) * entering


def finish_call(intra, entering, decay3, mixing3, gated, first, skip):
    tokens, channels = gated.shape
    modes = decay3.shape[0]
    return pl.pallas_call(
        finish_kernel,
        out_shape=whole((tokens, channels), jnp.bfloat16),
        in_specs=in_vmem(7),
        out_specs=pl.BlockSpec(memory_space=pltpu.VMEM),
        scratch_shapes=[pltpu.VMEM((tokens, channels), jnp.float32)],
        cost_estimate=pl.CostEstimate(
            flops=2 * modes * tokens * channels, transcendentals=modes * CHUNK * channels,
            bytes_accessed=14 * tokens * channels,
        ),
    )(intra, entering, decay3, mixing3, gated, first, skip)


def chunk_states(ends, decay):
    step = jnp.exp(-float(CHUNK) * decay)
    carry = jnp.zeros_like(decay)
    entering = []
    for chunk in range(ends.shape[1]):
        entering.append(carry)
        carry = step * carry + ends[:, chunk]
    return jnp.stack(entering, axis=1), carry


def block_body(features, short_filter, decay_rate, residue, skip_gain, norm_gain, qkv_weight):
    tok_dev, _, channels = features.shape
    head_cols = qkv_weight.shape[2]
    shard_rows = lax.all_gather(qkv_weight, "ctx", axis=0, tiled=True)
    rim_rows = features[tok_dev - (TAPS - 1) :]
    before = from_behind(rim_rows, "ctx", 1)
    decay3 = decay_rate[:, None, :]
    mixing3 = residue[:, None, :]
    first, gated, ends = front_call(features, before, short_filter, decay3)
    entering, block_end = chunk_states(ends, decay_rate)
    history = exchange_history(block_end, decay_rate, tok_dev)
    intra = intra_call(gated, decay3, mixing3)
    chunks = tok_dev // CHUNK
    lead = jnp.exp(-float(CHUNK) * jnp.arange(chunks, dtype=jnp.float32)[None, :, None] * decay_rate[:, None, :])
    total_state = entering + lead * history[:, None, :]
    mixer = finish_call(intra, total_state, decay3, mixing3, gated, first, skip_gain[None])

    parts = lax.axis_size("tp")
    copies = jnp.broadcast_to(mixer[None], (parts, tok_dev, channels))
    gathered = lax.all_to_all(copies, "tp", 0, 2, tiled=True).reshape(tok_dev, parts * channels)
    as_float = gathered.astype(jnp.float32)
    inverse = lax.rsqrt(jnp.mean(as_float * as_float, axis=1, keepdims=True) + EPSILON)
    normed = (as_float * inverse * norm_gain[None]).astype(jnp.bfloat16)
    flat_rows = shard_rows.reshape(shard_rows.shape[0], 3 * head_cols)
    projected = jnp.dot(normed, flat_rows, preferred_element_type=jnp.float32).astype(jnp.bfloat16)
    heads = head_cols // HD
    query = projected[:, :head_cols].reshape(tok_dev, heads, HD)
    kv_pair = projected[:, head_cols:]
    blocks_kv = [kv_pair]
    for _ in range(WINDOW - 1):
        blocks_kv.append(from_behind(blocks_kv[-1], "ctx", 1))
    position = lax.axis_index("ctx")
    row_ids = jnp.arange(tok_dev)
    causal = row_ids[:, None] >= row_ids[None, :]
    score_list = []
    for lag_step in range(WINDOW):
        keys = blocks_kv[lag_step][:, :head_cols].reshape(tok_dev, heads, HD)
        scores = jnp.einsum(
            "thd,shd->hts", query, keys, preferred_element_type=jnp.float32
        ) / math.sqrt(HD)
        if lag_step == 0:
            allowed = causal
        else:
            allowed = jnp.broadcast_to(position >= lag_step, causal.shape)
        score_list.append(jnp.where(allowed[None], scores, -jnp.inf))
    peak = reduce(jnp.maximum, [jnp.max(entry, axis=2) for entry in score_list])
    total = jnp.zeros((heads, tok_dev), jnp.float32)
    output = jnp.zeros((tok_dev, heads, HD), jnp.float32)
    for lag_step in range(WINDOW):
        expo = jnp.exp(score_list[lag_step] - peak[:, :, None])
        total = total + jnp.sum(expo, axis=2)
        values = blocks_kv[lag_step][:, head_cols:].reshape(tok_dev, heads, HD)
        output = output + jnp.einsum(
            "hts,shd->thd", expo.astype(jnp.bfloat16), values, preferred_element_type=jnp.float32
        )
    attended = (output / total.T[:, :, None]).astype(jnp.bfloat16).reshape(tok_dev, head_cols)
    return (mixer, attended)


def solution(mesh):
    placed = (
        P("ctx", None, "tp"),
        P(None, None, "tp"),
        P(None, "tp"),
        P(None, "tp"),
        P("tp"),
        P(),
        P("ctx", None, "tp"),
    )
    return jax.shard_map(
        block_body,
        mesh=mesh,
        in_specs=placed,
        out_specs=(P("ctx", "tp"), P("ctx", "tp")),
        check_vma=False,
    )
```

```python
from functools import reduce
import math

import jax
import jax.numpy as jnp
from jax import lax
from jax.sharding import PartitionSpec as P
from jax.experimental import pallas as pl
from jax.experimental.pallas import tpu as pltpu

HD = 128
TAPS = 7
WINDOW = 3
CHUNK = 128
GROUP = 8


EPSILON = 1e-06


def from_behind(value, axis, steps):
    count = lax.axis_size(axis)
    leading, last = (max(0, -steps), min(count, count - steps))
    return lax.ppermute(value, axis, [(source, source + steps) for source in range(leading, last)])


def bf16_split(value):
    high = value.astype(jnp.bfloat16)
    low = (value - high.astype(jnp.float32)).astype(jnp.bfloat16)
    return high, low


def intra_kernel(gated_ref, decay_ref, mixing_ref, intra_ref):
    tokens, channels = gated_ref.shape
    chunks = tokens // CHUNK
    offsets = lax.broadcasted_iota(jnp.int32, (CHUNK, channels), 0).astype(jnp.float32) - (CHUNK - 1) / 2.0
    rows = lax.broadcasted_iota(jnp.int32, (CHUNK, CHUNK), 0)
    cols = lax.broadcasted_iota(jnp.int32, (CHUNK, CHUNK), 1)
    tri = (rows >= cols).astype(jnp.float32).astype(jnp.bfloat16)
    intra_ref[...] = jnp.zeros_like(intra_ref)

    def add_mode(mode, unused):
        rate = decay_ref[mode]
        weight = mixing_ref[mode] * jnp.sqrt(rate)
        up = jnp.exp(offsets * rate)
        down = jnp.exp(-offsets * rate)
        for chunk in range(chunks):
            rows_of = pl.ds(chunk * CHUNK, CHUNK)
            high, low = bf16_split(up * gated_ref[rows_of, :])
            summed = jnp.dot(tri, high, preferred_element_type=jnp.float32) + jnp.dot(
                tri, low, preferred_element_type=jnp.float32
            )
            states = down * summed
            intra_ref[rows_of, :] += weight * states
        return unused

    lax.fori_loop(0, decay_ref.shape[0], add_mode, 0)


def front_kernel(feat_ref, halo_ref, taps_ref, decay_ref, first_ref, gated_ref, ends_ref, ext_ref):
    tokens, channels = first_ref.shape
    chunks = tokens // CHUNK
    lead = 8

    def short(stream, rows_of):
        taps = [taps_ref[stream, pl.ds(offset, 1), :] for offset in range(TAPS)]
        total = taps[0] * ext_ref[stream, pl.ds(lead + rows_of, CHUNK), :]
        for offset in range(1, TAPS):
            total = total + taps[offset] * ext_ref[stream, pl.ds(lead - offset + rows_of, CHUNK), :]
        return total

    for stream in range(3):
        cols = pl.ds(stream * channels, channels)
        ext_ref[stream, pl.ds(lead - (TAPS - 1), TAPS - 1), :] = halo_ref[:, cols].astype(jnp.float32)
        ext_ref[stream, pl.ds(lead, tokens), :] = feat_ref[:, cols].astype(jnp.float32)
    for chunk in range(chunks):
        rows_of = chunk * CHUNK
        first_ref[pl.ds(rows_of, CHUNK), :] = short(0, rows_of)
        product = short(1, rows_of) * short(2, rows_of)
        gated_ref[pl.ds(rows_of, CHUNK), :] = product.astype(jnp.bfloat16).astype(jnp.float32)

    tail = (CHUNK - 1) - lax.broadcasted_iota(jnp.int32, (CHUNK, channels), 0).astype(jnp.float32)

    def add_mode(mode, unused):
        fade = jnp.exp(-tail * decay_ref[mode])
        for chunk in range(chunks):
            block = gated_ref[pl.ds(chunk * CHUNK, CHUNK), :]
            ends_ref[mode, pl.ds(chunk, 1), :] = jnp.sum(fade * block, axis=0, keepdims=True)
        return unused

    lax.fori_loop(0, decay_ref.shape[0], add_mode, 0)


def front_call(features, halo, short_filter, decay3):
    tokens, streams, channels = features.shape
    modes = decay3.shape[0]
    chunks = tokens // CHUNK
    return pl.pallas_call(
        front_kernel,
        out_shape=(
            whole((tokens, channels), jnp.float32),
            whole((tokens, channels), jnp.float32),
            whole((modes, chunks, channels), jnp.float32),
        ),
        in_specs=in_vmem(4),
        out_specs=tuple(in_vmem(3)),
        scratch_shapes=[pltpu.VMEM((streams, tokens + 8, channels), jnp.float32)],
        cost_estimate=pl.CostEstimate(
            flops=2 * (3 * TAPS + modes) * tokens * channels, transcendentals=modes * CHUNK * channels,
            bytes_accessed=14 * tokens * channels,
        ),
    )(features.reshape(tokens, streams * channels), halo.reshape(halo.shape[0], streams * channels), short_filter, decay3)


def finish_kernel(intra_ref, state_ref, decay_ref, mixing_ref, gated_ref, first_ref, skip_ref, mixer_ref, acc_ref):
    tokens, channels = gated_ref.shape
    chunks = tokens // CHUNK
    after = lax.broadcasted_iota(jnp.int32, (CHUNK, channels), 0).astype(jnp.float32) + 1.0
    acc_ref[...] = intra_ref[...]

    def add_mode(mode, unused):
        rate = decay_ref[mode]
        decayed = jnp.exp(-after * rate) * (mixing_ref[mode] * jnp.sqrt(rate))
        for chunk in range(chunks):
            rows_of = pl.ds(chunk * CHUNK, CHUNK)
            acc_ref[rows_of, :] += decayed * state_ref[mode, pl.ds(chunk, 1), :]
        return unused

    lax.fori_loop(0, decay_ref.shape[0], add_mode, 0)
    filtered = acc_ref[...] + skip_ref[...] * gated_ref[...]
    filtered = filtered.astype(jnp.bfloat16).astype(jnp.float32)
    mixer_ref[...] = (first_ref[...] * filtered).astype(mixer_ref.dtype)


def whole(shape, dtype):
    return jax.ShapeDtypeStruct(shape, dtype)


def in_vmem(count):
    return [pl.BlockSpec(memory_space=pltpu.VMEM)] * count


def intra_call(gated, decay3, mixing3):
    tokens, channels = gated.shape
    modes = decay3.shape[0]
    return pl.pallas_call(
        intra_kernel,
        out_shape=whole((tokens, channels), jnp.float32),
        in_specs=in_vmem(3),
        out_specs=pl.BlockSpec(memory_space=pltpu.VMEM),
        cost_estimate=pl.CostEstimate(
            flops=4 * modes * tokens * CHUNK * channels, transcendentals=2 * modes * CHUNK * channels,
            bytes_accessed=8 * tokens * channels,
        ),
    )(gated, decay3, mixing3)


def exchange_history(block_end, decay, tok_dev):
    count = lax.axis_size("ctx")
    group = math.gcd(count, GROUP)
    me = lax.axis_index("ctx")
    place = me % group

    def decayed(blocks):
        return jnp.exp(-(blocks.astype(jnp.float32) * float(tok_dev)) * decay)

    prefix = jnp.zeros_like(decay)
    total = decayed(group - 1 - place) * block_end
    for shift in range(1, group):
        pairs = [(g + q, g + (q + shift) % group) for g in range(0, count, group) for q in range(group)]
        arrived = lax.ppermute(block_end, "ctx", pairs)
        source = (place - shift) % group
        prefix = prefix + jnp.where(source < place, decayed(place - 1 - source), 0.0) * arrived
        total = total + decayed(group - 1 - source) * arrived
    entering = jnp.zeros_like(decay)
    for hop in range(1, count // group):
        arrived = from_behind(total, "ctx", hop * group)
        entering = entering + decayed(jnp.int32((hop - 1) * group)) * arrived
    return prefix + decayed(place) * entering


def finish_call(intra, entering, decay3, mixing3, gated, first, skip):
    tokens, channels = gated.shape
    modes = decay3.shape[0]
    return pl.pallas_call(
        finish_kernel,
        out_shape=whole((tokens, channels), jnp.bfloat16),
        in_specs=in_vmem(7),
        out_specs=pl.BlockSpec(memory_space=pltpu.VMEM),
        scratch_shapes=[pltpu.VMEM((tokens, channels), jnp.float32)],
        cost_estimate=pl.CostEstimate(
            flops=2 * modes * tokens * channels, transcendentals=modes * CHUNK * channels,
            bytes_accessed=14 * tokens * channels,
        ),
    )(intra, entering, decay3, mixing3, gated, first, skip)


def chunk_states(ends, decay):
    step = jnp.exp(-float(CHUNK) * decay)
    carry = jnp.zeros_like(decay)
    entering = []
    for chunk in range(ends.shape[1]):
        entering.append(carry)
        carry = step * carry + ends[:, chunk]
    return jnp.stack(entering, axis=1), carry


def block_body(features, short_filter, decay_rate, residue, skip_gain, norm_gain, qkv_weight):
    tok_dev, _, channels = features.shape
    head_cols = qkv_weight.shape[2]
    shard_rows = lax.all_gather(qkv_weight, "ctx", axis=0, tiled=True)
    flat_rows = shard_rows.reshape(shard_rows.shape[0], 3 * head_cols)
    rim_rows = features[tok_dev - (TAPS - 1) :]
    before = from_behind(rim_rows, "ctx", 1)
    decay3 = decay_rate[:, None, :]
    mixing3 = residue[:, None, :]
    first, gated, ends = front_call(features, before, short_filter, decay3)
    entering, block_end = chunk_states(ends, decay_rate)
    history = exchange_history(block_end, decay_rate, tok_dev)
    intra = intra_call(gated, decay3, mixing3)
    chunks = tok_dev // CHUNK
    lead = jnp.exp(-float(CHUNK) * jnp.arange(chunks, dtype=jnp.float32)[None, :, None] * decay_rate[:, None, :])
    total_state = entering + lead * history[:, None, :]
    mixer = finish_call(intra, total_state, decay3, mixing3, gated, first, skip_gain[None])

    parts = lax.axis_size("tp")
    half = tok_dev // 4
    gathered_top = lax.all_gather(mixer[:half], "tp", axis=1, tiled=True)
    copies = jnp.broadcast_to(mixer[None, half:], (parts, tok_dev - half, channels))
    gathered_low = lax.all_to_all(copies, "tp", 0, 2, tiled=True).reshape(tok_dev - half, parts * channels)

    def project(gathered):
        as_float = gathered.astype(jnp.float32)
        inverse = lax.rsqrt(jnp.mean(as_float * as_float, axis=1, keepdims=True) + EPSILON)
        normed = (as_float * inverse * norm_gain[None]).astype(jnp.bfloat16)
        return jnp.dot(normed, flat_rows, preferred_element_type=jnp.float32).astype(jnp.bfloat16)

    projected = jnp.concatenate([project(gathered_top), project(gathered_low)], axis=0)
    heads = head_cols // HD
    query = projected[:, :head_cols].reshape(tok_dev, heads, HD)
    kv_pair = projected[:, head_cols:]
    blocks_kv = [kv_pair]
    for _ in range(WINDOW - 1):
        blocks_kv.append(from_behind(blocks_kv[-1], "ctx", 1))
    position = lax.axis_index("ctx")
    row_ids = jnp.arange(tok_dev)
    causal = row_ids[:, None] >= row_ids[None, :]
    score_list = []
    for lag_step in range(WINDOW):
        keys = blocks_kv[lag_step][:, :head_cols].reshape(tok_dev, heads, HD)
        scores = jnp.einsum(
            "thd,shd->hts", query, keys, preferred_element_type=jnp.float32
        ) / math.sqrt(HD)
        if lag_step == 0:
            allowed = causal
        else:
            allowed = jnp.broadcast_to(position >= lag_step, causal.shape)
        score_list.append(jnp.where(allowed[None], scores, -jnp.inf))
    peak = reduce(jnp.maximum, [jnp.max(entry, axis=2) for entry in score_list])
    total = jnp.zeros((heads, tok_dev), jnp.float32)
    output = jnp.zeros((tok_dev, heads, HD), jnp.float32)
    for lag_step in range(WINDOW):
        expo = jnp.exp(score_list[lag_step] - peak[:, :, None])
        total = total + jnp.sum(expo, axis=2)
        values = blocks_kv[lag_step][:, head_cols:].reshape(tok_dev, heads, HD)
        output = output + jnp.einsum(
            "hts,shd->thd", expo.astype(jnp.bfloat16), values, preferred_element_type=jnp.float32
        )
    attended = (output / total.T[:, :, None]).astype(jnp.bfloat16).reshape(tok_dev, head_cols)
    return (mixer, attended)


def solution(mesh):
    placed = (
        P("ctx", None, "tp"),
        P(None, None, "tp"),
        P(None, "tp"),
        P(None, "tp"),
        P("tp"),
        P(),
        P("ctx", None, "tp"),
    )
    return jax.shard_map(
        block_body,
        mesh=mesh,
        in_specs=placed,
        out_specs=(P("ctx", "tp"), P("ctx", "tp")),
        check_vma=False,
    )
```

```python
from functools import reduce
import math

import jax
import jax.numpy as jnp
from jax import lax
from jax.sharding import PartitionSpec as P
from jax.experimental import pallas as pl
from jax.experimental.pallas import tpu as pltpu

HD = 128
TAPS = 7
WINDOW = 3
CHUNK = 128
GROUP = 8


EPSILON = 1e-06


def from_behind(value, axis, steps):
    count = lax.axis_size(axis)
    leading, last = (max(0, -steps), min(count, count - steps))
    return lax.ppermute(value, axis, [(source, source + steps) for source in range(leading, last)])


def bf16_split(value):
    high = value.astype(jnp.bfloat16)
    low = (value - high.astype(jnp.float32)).astype(jnp.bfloat16)
    return high, low


def intra_kernel(gated_ref, decay_ref, mixing_ref, intra_ref):
    tokens, channels = gated_ref.shape
    chunks = tokens // CHUNK
    offsets = lax.broadcasted_iota(jnp.int32, (CHUNK, channels), 0).astype(jnp.float32) - (CHUNK - 1) / 2.0
    rows = lax.broadcasted_iota(jnp.int32, (CHUNK, CHUNK), 0)
    cols = lax.broadcasted_iota(jnp.int32, (CHUNK, CHUNK), 1)
    tri = (rows >= cols).astype(jnp.float32).astype(jnp.bfloat16)
    intra_ref[...] = jnp.zeros_like(intra_ref)

    def add_mode(mode, unused):
        rate = decay_ref[mode]
        weight = mixing_ref[mode] * jnp.sqrt(rate)
        up = jnp.exp(offsets * rate)
        down = jnp.exp(-offsets * rate)
        for chunk in range(chunks):
            rows_of = pl.ds(chunk * CHUNK, CHUNK)
            high, low = bf16_split(up * gated_ref[rows_of, :])
            summed = jnp.dot(tri, high, preferred_element_type=jnp.float32) + jnp.dot(
                tri, low, preferred_element_type=jnp.float32
            )
            states = down * summed
            intra_ref[rows_of, :] += weight * states
        return unused

    lax.fori_loop(0, decay_ref.shape[0], add_mode, 0)


def front_kernel(feat_ref, halo_ref, taps_ref, decay_ref, first_ref, gated_ref, ends_ref, ext_ref):
    tokens, channels = first_ref.shape
    chunks = tokens // CHUNK
    lead = 8

    def short(stream, rows_of):
        taps = [taps_ref[stream, pl.ds(offset, 1), :] for offset in range(TAPS)]
        total = taps[0] * ext_ref[stream, pl.ds(lead + rows_of, CHUNK), :]
        for offset in range(1, TAPS):
            total = total + taps[offset] * ext_ref[stream, pl.ds(lead - offset + rows_of, CHUNK), :]
        return total

    for stream in range(3):
        cols = pl.ds(stream * channels, channels)
        ext_ref[stream, pl.ds(lead - (TAPS - 1), TAPS - 1), :] = halo_ref[:, cols].astype(jnp.float32)
        ext_ref[stream, pl.ds(lead, tokens), :] = feat_ref[:, cols].astype(jnp.float32)
    for chunk in range(chunks):
        rows_of = chunk * CHUNK
        first_ref[pl.ds(rows_of, CHUNK), :] = short(0, rows_of)
        product = short(1, rows_of) * short(2, rows_of)
        gated_ref[pl.ds(rows_of, CHUNK), :] = product.astype(jnp.bfloat16).astype(jnp.float32)

    tail = (CHUNK - 1) - lax.broadcasted_iota(jnp.int32, (CHUNK, channels), 0).astype(jnp.float32)

    def add_mode(mode, unused):
        fade = jnp.exp(-tail * decay_ref[mode])
        for chunk in range(chunks):
            block = gated_ref[pl.ds(chunk * CHUNK, CHUNK), :]
            ends_ref[mode, pl.ds(chunk, 1), :] = jnp.sum(fade * block, axis=0, keepdims=True)
        return unused

    lax.fori_loop(0, decay_ref.shape[0], add_mode, 0)


def front_call(features, halo, short_filter, decay3):
    tokens, streams, channels = features.shape
    modes = decay3.shape[0]
    chunks = tokens // CHUNK
    return pl.pallas_call(
        front_kernel,
        out_shape=(
            whole((tokens, channels), jnp.float32),
            whole((tokens, channels), jnp.float32),
            whole((modes, chunks, channels), jnp.float32),
        ),
        in_specs=in_vmem(4),
        out_specs=tuple(in_vmem(3)),
        scratch_shapes=[pltpu.VMEM((streams, tokens + 8, channels), jnp.float32)],
        cost_estimate=pl.CostEstimate(
            flops=2 * (3 * TAPS + modes) * tokens * channels, transcendentals=modes * CHUNK * channels,
            bytes_accessed=14 * tokens * channels,
        ),
    )(features.reshape(tokens, streams * channels), halo.reshape(halo.shape[0], streams * channels), short_filter, decay3)


def finish_kernel(intra_ref, state_ref, decay_ref, mixing_ref, gated_ref, first_ref, skip_ref, mixer_ref, acc_ref):
    tokens, channels = gated_ref.shape
    chunks = tokens // CHUNK
    after = lax.broadcasted_iota(jnp.int32, (CHUNK, channels), 0).astype(jnp.float32) + 1.0
    acc_ref[...] = intra_ref[...]

    def add_mode(mode, unused):
        rate = decay_ref[mode]
        decayed = jnp.exp(-after * rate) * (mixing_ref[mode] * jnp.sqrt(rate))
        for chunk in range(chunks):
            rows_of = pl.ds(chunk * CHUNK, CHUNK)
            acc_ref[rows_of, :] += decayed * state_ref[mode, pl.ds(chunk, 1), :]
        return unused

    lax.fori_loop(0, decay_ref.shape[0], add_mode, 0)
    filtered = acc_ref[...] + skip_ref[...] * gated_ref[...]
    filtered = filtered.astype(jnp.bfloat16).astype(jnp.float32)
    mixer_ref[...] = (first_ref[...] * filtered).astype(mixer_ref.dtype)


def whole(shape, dtype):
    return jax.ShapeDtypeStruct(shape, dtype)


def in_vmem(count):
    return [pl.BlockSpec(memory_space=pltpu.VMEM)] * count


def intra_call(gated, decay3, mixing3):
    tokens, channels = gated.shape
    modes = decay3.shape[0]
    return pl.pallas_call(
        intra_kernel,
        out_shape=whole((tokens, channels), jnp.float32),
        in_specs=in_vmem(3),
        out_specs=pl.BlockSpec(memory_space=pltpu.VMEM),
        cost_estimate=pl.CostEstimate(
            flops=4 * modes * tokens * CHUNK * channels, transcendentals=2 * modes * CHUNK * channels,
            bytes_accessed=8 * tokens * channels,
        ),
    )(gated, decay3, mixing3)


def exchange_history(block_end, decay, tok_dev):
    count = lax.axis_size("ctx")
    group = math.gcd(count, GROUP)
    me = lax.axis_index("ctx")
    place = me % group

    def decayed(blocks):
        return jnp.exp(-(blocks.astype(jnp.float32) * float(tok_dev)) * decay)

    prefix = jnp.zeros_like(decay)
    total = decayed(group - 1 - place) * block_end
    for shift in range(1, group):
        pairs = [(g + q, g + (q + shift) % group) for g in range(0, count, group) for q in range(group)]
        arrived = lax.ppermute(block_end, "ctx", pairs)
        source = (place - shift) % group
        prefix = prefix + jnp.where(source < place, decayed(place - 1 - source), 0.0) * arrived
        total = total + decayed(group - 1 - source) * arrived
    entering = jnp.zeros_like(decay)
    for hop in range(1, count // group):
        arrived = from_behind(total, "ctx", hop * group)
        entering = entering + decayed(jnp.int32((hop - 1) * group)) * arrived
    return prefix + decayed(place) * entering


def finish_call(intra, entering, decay3, mixing3, gated, first, skip):
    tokens, channels = gated.shape
    modes = decay3.shape[0]
    return pl.pallas_call(
        finish_kernel,
        out_shape=whole((tokens, channels), jnp.bfloat16),
        in_specs=in_vmem(7),
        out_specs=pl.BlockSpec(memory_space=pltpu.VMEM),
        scratch_shapes=[pltpu.VMEM((tokens, channels), jnp.float32)],
        cost_estimate=pl.CostEstimate(
            flops=2 * modes * tokens * channels, transcendentals=modes * CHUNK * channels,
            bytes_accessed=14 * tokens * channels,
        ),
    )(intra, entering, decay3, mixing3, gated, first, skip)


def chunk_states(ends, decay):
    step = jnp.exp(-float(CHUNK) * decay)
    carry = jnp.zeros_like(decay)
    entering = []
    for chunk in range(ends.shape[1]):
        entering.append(carry)
        carry = step * carry + ends[:, chunk]
    return jnp.stack(entering, axis=1), carry


def block_body(features, short_filter, decay_rate, residue, skip_gain, norm_gain, qkv_weight):
    tok_dev, _, channels = features.shape
    head_cols = qkv_weight.shape[2]
    shard_rows = lax.all_gather(qkv_weight, "ctx", axis=0, tiled=True)
    rim_rows = features[tok_dev - (TAPS - 1) :]
    before = from_behind(rim_rows, "ctx", 1)
    decay3 = decay_rate[:, None, :]
    mixing3 = residue[:, None, :]
    first, gated, ends = front_call(features, before, short_filter, decay3)
    entering, block_end = chunk_states(ends, decay_rate)
    history = exchange_history(block_end, decay_rate, tok_dev)
    intra = intra_call(gated, decay3, mixing3)
    chunks = tok_dev // CHUNK
    lead = jnp.exp(-float(CHUNK) * jnp.arange(chunks, dtype=jnp.float32)[None, :, None] * decay_rate[:, None, :])
    total_state = entering + lead * history[:, None, :]
    mixer = finish_call(intra, total_state, decay3, mixing3, gated, first, skip_gain[None])

    parts = lax.axis_size("tp")
    me = lax.axis_index("tp")
    pieces = [mixer] + [
        lax.ppermute(mixer, "tp", [((source + shift) % parts, source) for source in range(parts)])
        for shift in range(1, parts)
    ]
    doubled = jnp.concatenate(pieces + pieces, axis=1)
    gathered = lax.dynamic_slice_in_dim(doubled, ((parts - me) % parts) * channels, parts * channels, 1)
    as_float = gathered.astype(jnp.float32)
    inverse = lax.rsqrt(jnp.mean(as_float * as_float, axis=1, keepdims=True) + EPSILON)
    normed = (as_float * inverse * norm_gain[None]).astype(jnp.bfloat16)
    flat_rows = shard_rows.reshape(shard_rows.shape[0], 3 * head_cols)
    kv_pair = jnp.dot(normed, flat_rows[:, head_cols:], preferred_element_type=jnp.float32).astype(jnp.bfloat16)
    heads = head_cols // HD
    blocks_kv = [kv_pair]
    for _ in range(WINDOW - 1):
        blocks_kv.append(from_behind(blocks_kv[-1], "ctx", 1))
    projected_q = jnp.dot(normed, flat_rows[:, :head_cols], preferred_element_type=jnp.float32).astype(jnp.bfloat16)
    query = projected_q.reshape(tok_dev, heads, HD)
    position = lax.axis_index("ctx")
    row_ids = jnp.arange(tok_dev)
    causal = row_ids[:, None] >= row_ids[None, :]
    score_list = []
    for lag_step in range(WINDOW):
        keys = blocks_kv[lag_step][:, :head_cols].reshape(tok_dev, heads, HD)
        scores = jnp.einsum(
            "thd,shd->hts", query, keys, preferred_element_type=jnp.float32
        ) / math.sqrt(HD)
        if lag_step == 0:
            allowed = causal
        else:
            allowed = jnp.broadcast_to(position >= lag_step, causal.shape)
        score_list.append(jnp.where(allowed[None], scores, -jnp.inf))
    peak = reduce(jnp.maximum, [jnp.max(entry, axis=2) for entry in score_list])
    total = jnp.zeros((heads, tok_dev), jnp.float32)
    output = jnp.zeros((tok_dev, heads, HD), jnp.float32)
    for lag_step in range(WINDOW):
        expo = jnp.exp(score_list[lag_step] - peak[:, :, None])
        total = total + jnp.sum(expo, axis=2)
        values = blocks_kv[lag_step][:, head_cols:].reshape(tok_dev, heads, HD)
        output = output + jnp.einsum(
            "hts,shd->thd", expo.astype(jnp.bfloat16), values, preferred_element_type=jnp.float32
        )
    attended = (output / total.T[:, :, None]).astype(jnp.bfloat16).reshape(tok_dev, head_cols)
    return (mixer, attended)


def solution(mesh):
    placed = (
        P("ctx", None, "tp"),
        P(None, None, "tp"),
        P(None, "tp"),
        P(None, "tp"),
        P("tp"),
        P(),
        P("ctx", None, "tp"),
    )
    return jax.shard_map(
        block_body,
        mesh=mesh,
        in_specs=placed,
        out_specs=(P("ctx", "tp"), P("ctx", "tp")),
        check_vma=False,
    )
```

```python
from functools import reduce
import math

import jax
import jax.numpy as jnp
from jax import lax
from jax.sharding import PartitionSpec as P
from jax.experimental import pallas as pl
from jax.experimental.pallas import tpu as pltpu

HD = 128
TAPS = 7
WINDOW = 3
CHUNK = 128
GROUP = 8


EPSILON = 1e-06


def from_behind(value, axis, steps):
    count = lax.axis_size(axis)
    leading, last = (max(0, -steps), min(count, count - steps))
    return lax.ppermute(value, axis, [(source, source + steps) for source in range(leading, last)])


def bf16_split(value):
    high = value.astype(jnp.bfloat16)
    low = (value - high.astype(jnp.float32)).astype(jnp.bfloat16)
    return high, low


def intra_kernel(gated_ref, decay_ref, mixing_ref, intra_ref):
    tokens, channels = gated_ref.shape
    chunks = tokens // CHUNK
    offsets = lax.broadcasted_iota(jnp.int32, (CHUNK, channels), 0).astype(jnp.float32) - (CHUNK - 1) / 2.0
    rows = lax.broadcasted_iota(jnp.int32, (CHUNK, CHUNK), 0)
    cols = lax.broadcasted_iota(jnp.int32, (CHUNK, CHUNK), 1)
    tri = (rows >= cols).astype(jnp.float32).astype(jnp.bfloat16)
    intra_ref[...] = jnp.zeros_like(intra_ref)

    def add_mode(mode, unused):
        rate = decay_ref[mode]
        weight = mixing_ref[mode] * jnp.sqrt(rate)
        up = jnp.exp(offsets * rate)
        down = jnp.exp(-offsets * rate)
        for chunk in range(chunks):
            rows_of = pl.ds(chunk * CHUNK, CHUNK)
            high, low = bf16_split(up * gated_ref[rows_of, :])
            summed = jnp.dot(tri, high, preferred_element_type=jnp.float32) + jnp.dot(
                tri, low, preferred_element_type=jnp.float32
            )
            states = down * summed
            intra_ref[rows_of, :] += weight * states
        return unused

    lax.fori_loop(0, decay_ref.shape[0], add_mode, 0)


def front_kernel(feat_ref, halo_ref, taps_ref, decay_ref, first_ref, gated_ref, ends_ref, ext_ref):
    tokens, channels = first_ref.shape
    chunks = tokens // CHUNK
    lead = 8

    def short(stream, rows_of):
        taps = [taps_ref[stream, pl.ds(offset, 1), :] for offset in range(TAPS)]
        total = taps[0] * ext_ref[stream, pl.ds(lead + rows_of, CHUNK), :]
        for offset in range(1, TAPS):
            total = total + taps[offset] * ext_ref[stream, pl.ds(lead - offset + rows_of, CHUNK), :]
        return total

    for stream in range(3):
        cols = pl.ds(stream * channels, channels)
        ext_ref[stream, pl.ds(lead - (TAPS - 1), TAPS - 1), :] = halo_ref[:, cols].astype(jnp.float32)
        ext_ref[stream, pl.ds(lead, tokens), :] = feat_ref[:, cols].astype(jnp.float32)
    for chunk in range(chunks):
        rows_of = chunk * CHUNK
        first_ref[pl.ds(rows_of, CHUNK), :] = short(0, rows_of)
        product = short(1, rows_of) * short(2, rows_of)
        gated_ref[pl.ds(rows_of, CHUNK), :] = product.astype(jnp.bfloat16).astype(jnp.float32)

    tail = (CHUNK - 1) - lax.broadcasted_iota(jnp.int32, (CHUNK, channels), 0).astype(jnp.float32)

    def add_mode(mode, unused):
        fade = jnp.exp(-tail * decay_ref[mode])
        for chunk in range(chunks):
            block = gated_ref[pl.ds(chunk * CHUNK, CHUNK), :]
            ends_ref[mode, pl.ds(chunk, 1), :] = jnp.sum(fade * block, axis=0, keepdims=True)
        return unused

    lax.fori_loop(0, decay_ref.shape[0], add_mode, 0)


def front_call(features, halo, short_filter, decay3):
    tokens, streams, channels = features.shape
    modes = decay3.shape[0]
    chunks = tokens // CHUNK
    return pl.pallas_call(
        front_kernel,
        out_shape=(
            whole((tokens, channels), jnp.float32),
            whole((tokens, channels), jnp.float32),
            whole((modes, chunks, channels), jnp.float32),
        ),
        in_specs=in_vmem(4),
        out_specs=tuple(in_vmem(3)),
        scratch_shapes=[pltpu.VMEM((streams, tokens + 8, channels), jnp.float32)],
        cost_estimate=pl.CostEstimate(
            flops=2 * (3 * TAPS + modes) * tokens * channels, transcendentals=modes * CHUNK * channels,
            bytes_accessed=14 * tokens * channels,
        ),
    )(features.reshape(tokens, streams * channels), halo.reshape(halo.shape[0], streams * channels), short_filter, decay3)


def finish_kernel(intra_ref, state_ref, decay_ref, mixing_ref, gated_ref, first_ref, skip_ref, mixer_ref, acc_ref):
    tokens, channels = gated_ref.shape
    chunks = tokens // CHUNK
    after = lax.broadcasted_iota(jnp.int32, (CHUNK, channels), 0).astype(jnp.float32) + 1.0
    acc_ref[...] = intra_ref[...]

    def add_mode(mode, unused):
        rate = decay_ref[mode]
        decayed = jnp.exp(-after * rate) * (mixing_ref[mode] * jnp.sqrt(rate))
        for chunk in range(chunks):
            rows_of = pl.ds(chunk * CHUNK, CHUNK)
            acc_ref[rows_of, :] += decayed * state_ref[mode, pl.ds(chunk, 1), :]
        return unused

    lax.fori_loop(0, decay_ref.shape[0], add_mode, 0)
    filtered = acc_ref[...] + skip_ref[...] * gated_ref[...]
    filtered = filtered.astype(jnp.bfloat16).astype(jnp.float32)
    mixer_ref[...] = (first_ref[...] * filtered).astype(mixer_ref.dtype)


def whole(shape, dtype):
    return jax.ShapeDtypeStruct(shape, dtype)


def in_vmem(count):
    return [pl.BlockSpec(memory_space=pltpu.VMEM)] * count


def intra_call(gated, decay3, mixing3):
    tokens, channels = gated.shape
    modes = decay3.shape[0]
    return pl.pallas_call(
        intra_kernel,
        out_shape=whole((tokens, channels), jnp.float32),
        in_specs=in_vmem(3),
        out_specs=pl.BlockSpec(memory_space=pltpu.VMEM),
        cost_estimate=pl.CostEstimate(
            flops=4 * modes * tokens * CHUNK * channels, transcendentals=2 * modes * CHUNK * channels,
            bytes_accessed=8 * tokens * channels,
        ),
    )(gated, decay3, mixing3)


def exchange_history(block_end, decay, tok_dev):
    count = lax.axis_size("ctx")
    group = math.gcd(count, GROUP)
    me = lax.axis_index("ctx")
    place = me % group

    def decayed(blocks):
        return jnp.exp(-(blocks.astype(jnp.float32) * float(tok_dev)) * decay)

    prefix = jnp.zeros_like(decay)
    total = decayed(group - 1 - place) * block_end
    for shift in range(1, group):
        pairs = [(g + q, g + (q + shift) % group) for g in range(0, count, group) for q in range(group)]
        arrived = lax.ppermute(block_end, "ctx", pairs)
        source = (place - shift) % group
        prefix = prefix + jnp.where(source < place, decayed(place - 1 - source), 0.0) * arrived
        total = total + decayed(group - 1 - source) * arrived
    entering = jnp.zeros_like(decay)
    for hop in range(1, count // group):
        arrived = from_behind(total, "ctx", hop * group)
        entering = entering + decayed(jnp.int32((hop - 1) * group)) * arrived
    return prefix + decayed(place) * entering


def finish_call(intra, entering, decay3, mixing3, gated, first, skip):
    tokens, channels = gated.shape
    modes = decay3.shape[0]
    return pl.pallas_call(
        finish_kernel,
        out_shape=whole((tokens, channels), jnp.bfloat16),
        in_specs=in_vmem(7),
        out_specs=pl.BlockSpec(memory_space=pltpu.VMEM),
        scratch_shapes=[pltpu.VMEM((tokens, channels), jnp.float32)],
        cost_estimate=pl.CostEstimate(
            flops=2 * modes * tokens * channels, transcendentals=modes * CHUNK * channels,
            bytes_accessed=14 * tokens * channels,
        ),
    )(intra, entering, decay3, mixing3, gated, first, skip)


def chunk_states(ends, decay):
    step = jnp.exp(-float(CHUNK) * decay)
    carry = jnp.zeros_like(decay)
    entering = []
    for chunk in range(ends.shape[1]):
        entering.append(carry)
        carry = step * carry + ends[:, chunk]
    return jnp.stack(entering, axis=1), carry


def block_body(features, short_filter, decay_rate, residue, skip_gain, norm_gain, qkv_weight):
    tok_dev, _, channels = features.shape
    head_cols = qkv_weight.shape[2]
    shard_rows = lax.all_gather(qkv_weight, "ctx", axis=0, tiled=True)
    rim_rows = features[tok_dev - (TAPS - 1) :]
    before = from_behind(rim_rows, "ctx", 1)
    decay3 = decay_rate[:, None, :]
    mixing3 = residue[:, None, :]
    first, gated, ends = front_call(features, before, short_filter, decay3)
    entering, block_end = chunk_states(ends, decay_rate)
    history = exchange_history(block_end, decay_rate, tok_dev)
    intra = intra_call(gated, decay3, mixing3)
    chunks = tok_dev // CHUNK
    lead = jnp.exp(-float(CHUNK) * jnp.arange(chunks, dtype=jnp.float32)[None, :, None] * decay_rate[:, None, :])
    total_state = entering + lead * history[:, None, :]
    mixer = finish_call(intra, total_state, decay3, mixing3, gated, first, skip_gain[None])

    parts = lax.axis_size("tp")
    me = lax.axis_index("tp")
    pieces = [mixer] + [
        lax.ppermute(mixer, "tp", [((source + shift) % parts, source) for source in range(parts)])
        for shift in range(1, parts)
    ]
    doubled = jnp.concatenate(pieces + pieces, axis=1)
    gathered = lax.dynamic_slice_in_dim(doubled, ((parts - me) % parts) * channels, parts * channels, 1)
    as_float = gathered.astype(jnp.float32)
    inverse = lax.rsqrt(jnp.mean(as_float * as_float, axis=1, keepdims=True) + EPSILON)
    normed = (as_float * inverse * norm_gain[None]).astype(jnp.bfloat16)
    flat_rows = shard_rows.reshape(shard_rows.shape[0], 3 * head_cols)
    kv_pair = jnp.dot(normed, flat_rows[:, head_cols:], preferred_element_type=jnp.float32).astype(jnp.bfloat16)
    heads = head_cols // HD
    blocks_k = [kv_pair[:, :head_cols]]
    blocks_v = [kv_pair[:, head_cols:]]
    for _ in range(WINDOW - 1):
        blocks_k.append(from_behind(blocks_k[-1], "ctx", 1))
        blocks_v.append(from_behind(blocks_v[-1], "ctx", 1))
    projected_q = jnp.dot(normed, flat_rows[:, :head_cols], preferred_element_type=jnp.float32).astype(jnp.bfloat16)
    query = projected_q.reshape(tok_dev, heads, HD)
    position = lax.axis_index("ctx")
    row_ids = jnp.arange(tok_dev)
    causal = row_ids[:, None] >= row_ids[None, :]
    score_list = []
    for lag_step in range(WINDOW):
        keys = blocks_k[lag_step].reshape(tok_dev, heads, HD)
        scores = jnp.einsum(
            "thd,shd->hts", query, keys, preferred_element_type=jnp.float32
        ) / math.sqrt(HD)
        if lag_step == 0:
            allowed = causal
        else:
            allowed = jnp.broadcast_to(position >= lag_step, causal.shape)
        score_list.append(jnp.where(allowed[None], scores, -jnp.inf))
    peak = reduce(jnp.maximum, [jnp.max(entry, axis=2) for entry in score_list])
    total = jnp.zeros((heads, tok_dev), jnp.float32)
    output = jnp.zeros((tok_dev, heads, HD), jnp.float32)
    for lag_step in range(WINDOW):
        expo = jnp.exp(score_list[lag_step] - peak[:, :, None])
        total = total + jnp.sum(expo, axis=2)
        values = blocks_v[lag_step].reshape(tok_dev, heads, HD)
        output = output + jnp.einsum(
            "hts,shd->thd", expo.astype(jnp.bfloat16), values, preferred_element_type=jnp.float32
        )
    attended = (output / total.T[:, :, None]).astype(jnp.bfloat16).reshape(tok_dev, head_cols)
    return (mixer, attended)


def solution(mesh):
    placed = (
        P("ctx", None, "tp"),
        P(None, None, "tp"),
        P(None, "tp"),
        P(None, "tp"),
        P("tp"),
        P(),
        P("ctx", None, "tp"),
    )
    return jax.shard_map(
        block_body,
        mesh=mesh,
        in_specs=placed,
        out_specs=(P("ctx", "tp"), P("ctx", "tp")),
        check_vma=False,
    )
```

```python
from functools import reduce
import math

import jax
import jax.numpy as jnp
from jax import lax
from jax.sharding import PartitionSpec as P
from jax.experimental import pallas as pl
from jax.experimental.pallas import tpu as pltpu

HD = 128
TAPS = 7
WINDOW = 3
CHUNK = 128
GROUP = 8


EPSILON = 1e-06


def from_behind(value, axis, steps):
    count = lax.axis_size(axis)
    leading, last = (max(0, -steps), min(count, count - steps))
    return lax.ppermute(value, axis, [(source, source + steps) for source in range(leading, last)])


def bf16_split(value):
    high = value.astype(jnp.bfloat16)
    low = (value - high.astype(jnp.float32)).astype(jnp.bfloat16)
    return high, low


def intra_kernel(gated_ref, decay_ref, mixing_ref, intra_ref):
    tokens, channels = gated_ref.shape
    chunks = tokens // CHUNK
    offsets = lax.broadcasted_iota(jnp.int32, (CHUNK, channels), 0).astype(jnp.float32) - (CHUNK - 1) / 2.0
    rows = lax.broadcasted_iota(jnp.int32, (CHUNK, CHUNK), 0)
    cols = lax.broadcasted_iota(jnp.int32, (CHUNK, CHUNK), 1)
    tri = (rows >= cols).astype(jnp.float32).astype(jnp.bfloat16)
    intra_ref[...] = jnp.zeros_like(intra_ref)

    def add_mode(mode, unused):
        rate = decay_ref[mode]
        weight = mixing_ref[mode] * jnp.sqrt(rate)
        up = jnp.exp(offsets * rate)
        down = jnp.exp(-offsets * rate)
        for chunk in range(chunks):
            rows_of = pl.ds(chunk * CHUNK, CHUNK)
            high, low = bf16_split(up * gated_ref[rows_of, :])
            summed = jnp.dot(tri, high, preferred_element_type=jnp.float32) + jnp.dot(
                tri, low, preferred_element_type=jnp.float32
            )
            states = down * summed
            intra_ref[rows_of, :] += weight * states
        return unused

    lax.fori_loop(0, decay_ref.shape[0], add_mode, 0)


def front_kernel(feat_ref, halo_ref, taps_ref, decay_ref, first_ref, gated_ref, ends_ref, ext_ref):
    tokens, channels = first_ref.shape
    chunks = tokens // CHUNK
    lead = 8

    def short(stream, rows_of):
        taps = [taps_ref[stream, pl.ds(offset, 1), :] for offset in range(TAPS)]
        total = taps[0] * ext_ref[stream, pl.ds(lead + rows_of, CHUNK), :]
        for offset in range(1, TAPS):
            total = total + taps[offset] * ext_ref[stream, pl.ds(lead - offset + rows_of, CHUNK), :]
        return total

    for stream in range(3):
        cols = pl.ds(stream * channels, channels)
        ext_ref[stream, pl.ds(lead - (TAPS - 1), TAPS - 1), :] = halo_ref[:, cols].astype(jnp.float32)
        ext_ref[stream, pl.ds(lead, tokens), :] = feat_ref[:, cols].astype(jnp.float32)
    for chunk in range(chunks):
        rows_of = chunk * CHUNK
        first_ref[pl.ds(rows_of, CHUNK), :] = short(0, rows_of)
        product = short(1, rows_of) * short(2, rows_of)
        gated_ref[pl.ds(rows_of, CHUNK), :] = product.astype(jnp.bfloat16).astype(jnp.float32)

    tail = (CHUNK - 1) - lax.broadcasted_iota(jnp.int32, (CHUNK, channels), 0).astype(jnp.float32)

    def add_mode(mode, unused):
        fade = jnp.exp(-tail * decay_ref[mode])
        for chunk in range(chunks):
            block = gated_ref[pl.ds(chunk * CHUNK, CHUNK), :]
            ends_ref[mode, pl.ds(chunk, 1), :] = jnp.sum(fade * block, axis=0, keepdims=True)
        return unused

    lax.fori_loop(0, decay_ref.shape[0], add_mode, 0)


def front_call(features, halo, short_filter, decay3):
    tokens, streams, channels = features.shape
    modes = decay3.shape[0]
    chunks = tokens // CHUNK
    return pl.pallas_call(
        front_kernel,
        out_shape=(
            whole((tokens, channels), jnp.float32),
            whole((tokens, channels), jnp.float32),
            whole((modes, chunks, channels), jnp.float32),
        ),
        in_specs=in_vmem(4),
        out_specs=tuple(in_vmem(3)),
        scratch_shapes=[pltpu.VMEM((streams, tokens + 8, channels), jnp.float32)],
        cost_estimate=pl.CostEstimate(
            flops=2 * (3 * TAPS + modes) * tokens * channels, transcendentals=modes * CHUNK * channels,
            bytes_accessed=14 * tokens * channels,
        ),
    )(features.reshape(tokens, streams * channels), halo.reshape(halo.shape[0], streams * channels), short_filter, decay3)


def finish_kernel(intra_ref, state_ref, decay_ref, mixing_ref, gated_ref, first_ref, skip_ref, mixer_ref, acc_ref):
    tokens, channels = gated_ref.shape
    chunks = tokens // CHUNK
    after = lax.broadcasted_iota(jnp.int32, (CHUNK, channels), 0).astype(jnp.float32) + 1.0
    acc_ref[...] = intra_ref[...]

    def add_mode(mode, unused):
        rate = decay_ref[mode]
        decayed = jnp.exp(-after * rate) * (mixing_ref[mode] * jnp.sqrt(rate))
        for chunk in range(chunks):
            rows_of = pl.ds(chunk * CHUNK, CHUNK)
            acc_ref[rows_of, :] += decayed * state_ref[mode, pl.ds(chunk, 1), :]
        return unused

    lax.fori_loop(0, decay_ref.shape[0], add_mode, 0)
    filtered = acc_ref[...] + skip_ref[...] * gated_ref[...]
    filtered = filtered.astype(jnp.bfloat16).astype(jnp.float32)
    mixer_ref[...] = (first_ref[...] * filtered).astype(mixer_ref.dtype)


def whole(shape, dtype):
    return jax.ShapeDtypeStruct(shape, dtype)


def in_vmem(count):
    return [pl.BlockSpec(memory_space=pltpu.VMEM)] * count


def intra_call(gated, decay3, mixing3):
    tokens, channels = gated.shape
    modes = decay3.shape[0]
    return pl.pallas_call(
        intra_kernel,
        out_shape=whole((tokens, channels), jnp.float32),
        in_specs=in_vmem(3),
        out_specs=pl.BlockSpec(memory_space=pltpu.VMEM),
        cost_estimate=pl.CostEstimate(
            flops=4 * modes * tokens * CHUNK * channels, transcendentals=2 * modes * CHUNK * channels,
            bytes_accessed=8 * tokens * channels,
        ),
    )(gated, decay3, mixing3)


def exchange_history(block_end, decay, tok_dev):
    count = lax.axis_size("ctx")
    group = math.gcd(count, GROUP)
    me = lax.axis_index("ctx")
    place = me % group

    def decayed(blocks):
        return jnp.exp(-(blocks.astype(jnp.float32) * float(tok_dev)) * decay)

    prefix = jnp.zeros_like(decay)
    total = decayed(group - 1 - place) * block_end
    for shift in range(1, group):
        pairs = [(g + q, g + (q + shift) % group) for g in range(0, count, group) for q in range(group)]
        arrived = lax.ppermute(block_end, "ctx", pairs)
        source = (place - shift) % group
        prefix = prefix + jnp.where(source < place, decayed(place - 1 - source), 0.0) * arrived
        total = total + decayed(group - 1 - source) * arrived
    entering = jnp.zeros_like(decay)
    for hop in range(1, count // group):
        arrived = from_behind(total, "ctx", hop * group)
        entering = entering + decayed(jnp.int32((hop - 1) * group)) * arrived
    return prefix + decayed(place) * entering


def finish_call(intra, entering, decay3, mixing3, gated, first, skip):
    tokens, channels = gated.shape
    modes = decay3.shape[0]
    return pl.pallas_call(
        finish_kernel,
        out_shape=whole((tokens, channels), jnp.bfloat16),
        in_specs=in_vmem(7),
        out_specs=pl.BlockSpec(memory_space=pltpu.VMEM),
        scratch_shapes=[pltpu.VMEM((tokens, channels), jnp.float32)],
        cost_estimate=pl.CostEstimate(
            flops=2 * modes * tokens * channels, transcendentals=modes * CHUNK * channels,
            bytes_accessed=14 * tokens * channels,
        ),
    )(intra, entering, decay3, mixing3, gated, first, skip)


def chunk_states(ends, decay):
    step = jnp.exp(-float(CHUNK) * decay)
    carry = jnp.zeros_like(decay)
    entering = []
    for chunk in range(ends.shape[1]):
        entering.append(carry)
        carry = step * carry + ends[:, chunk]
    return jnp.stack(entering, axis=1), carry


def block_body(features, short_filter, decay_rate, residue, skip_gain, norm_gain, qkv_weight):
    tok_dev, _, channels = features.shape
    head_cols = qkv_weight.shape[2]
    shard_rows = lax.all_gather(qkv_weight, "ctx", axis=0, tiled=True)
    rim_rows = features[tok_dev - (TAPS - 1) :]
    before = from_behind(rim_rows, "ctx", 1)
    decay3 = decay_rate[:, None, :]
    mixing3 = residue[:, None, :]
    first, gated, ends = front_call(features, before, short_filter, decay3)
    entering, block_end = chunk_states(ends, decay_rate)
    history = exchange_history(block_end, decay_rate, tok_dev)
    intra = intra_call(gated, decay3, mixing3)
    chunks = tok_dev // CHUNK
    lead = jnp.exp(-float(CHUNK) * jnp.arange(chunks, dtype=jnp.float32)[None, :, None] * decay_rate[:, None, :])
    total_state = entering + lead * history[:, None, :]
    mixer = finish_call(intra, total_state, decay3, mixing3, gated, first, skip_gain[None])

    parts = lax.axis_size("tp")
    me = lax.axis_index("tp")
    pieces = [mixer] + [
        lax.ppermute(mixer, "tp", [((source + shift) % parts, source) for source in range(parts)])
        for shift in range(1, parts)
    ]
    doubled = jnp.concatenate(pieces + pieces, axis=1)
    gathered = lax.dynamic_slice_in_dim(doubled, ((parts - me) % parts) * channels, parts * channels, 1)
    as_float = gathered.astype(jnp.float32)
    inverse = lax.rsqrt(jnp.mean(as_float * as_float, axis=1, keepdims=True) + EPSILON)
    normed = (as_float * inverse * norm_gain[None]).astype(jnp.bfloat16)
    flat_rows = shard_rows.reshape(shard_rows.shape[0], 3 * head_cols)
    keys_own = jnp.dot(normed, flat_rows[:, head_cols : 2 * head_cols], preferred_element_type=jnp.float32)
    values_own = jnp.dot(normed, flat_rows[:, 2 * head_cols :], preferred_element_type=jnp.float32)
    heads = head_cols // HD
    blocks_k = [keys_own.astype(jnp.bfloat16)]
    blocks_v = [values_own.astype(jnp.bfloat16)]
    for _ in range(WINDOW - 1):
        blocks_k.append(from_behind(blocks_k[-1], "ctx", 1))
        blocks_v.append(from_behind(blocks_v[-1], "ctx", 1))
    projected_q = jnp.dot(normed, flat_rows[:, :head_cols], preferred_element_type=jnp.float32).astype(jnp.bfloat16)
    query = projected_q.reshape(tok_dev, heads, HD)
    position = lax.axis_index("ctx")
    row_ids = jnp.arange(tok_dev)
    causal = row_ids[:, None] >= row_ids[None, :]
    score_list = []
    for lag_step in range(WINDOW):
        keys = blocks_k[lag_step].reshape(tok_dev, heads, HD)
        scores = jnp.einsum(
            "thd,shd->hts", query, keys, preferred_element_type=jnp.float32
        ) / math.sqrt(HD)
        if lag_step == 0:
            allowed = causal
        else:
            allowed = jnp.broadcast_to(position >= lag_step, causal.shape)
        score_list.append(jnp.where(allowed[None], scores, -jnp.inf))
    peak = reduce(jnp.maximum, [jnp.max(entry, axis=2) for entry in score_list])
    total = jnp.zeros((heads, tok_dev), jnp.float32)
    output = jnp.zeros((tok_dev, heads, HD), jnp.float32)
    for lag_step in range(WINDOW):
        expo = jnp.exp(score_list[lag_step] - peak[:, :, None])
        total = total + jnp.sum(expo, axis=2)
        values = blocks_v[lag_step].reshape(tok_dev, heads, HD)
        output = output + jnp.einsum(
            "hts,shd->thd", expo.astype(jnp.bfloat16), values, preferred_element_type=jnp.float32
        )
    attended = (output / total.T[:, :, None]).astype(jnp.bfloat16).reshape(tok_dev, head_cols)
    return (mixer, attended)


def solution(mesh):
    placed = (
        P("ctx", None, "tp"),
        P(None, None, "tp"),
        P(None, "tp"),
        P(None, "tp"),
        P("tp"),
        P(),
        P("ctx", None, "tp"),
    )
    return jax.shard_map(
        block_body,
        mesh=mesh,
        in_specs=placed,
        out_specs=(P("ctx", "tp"), P("ctx", "tp")),
        check_vma=False,
    )
```

```python
from functools import reduce
import math

import jax
import jax.numpy as jnp
from jax import lax
from jax.sharding import PartitionSpec as P
from jax.experimental import pallas as pl
from jax.experimental.pallas import tpu as pltpu

HD = 128
TAPS = 7
WINDOW = 3
CHUNK = 128
GROUP = 8


EPSILON = 1e-06


def from_behind(value, axis, steps):
    count = lax.axis_size(axis)
    leading, last = (max(0, -steps), min(count, count - steps))
    return lax.ppermute(value, axis, [(source, source + steps) for source in range(leading, last)])


def bf16_split(value):
    high = value.astype(jnp.bfloat16)
    low = (value - high.astype(jnp.float32)).astype(jnp.bfloat16)
    return high, low


def intra_kernel(gated_ref, decay_ref, mixing_ref, intra_ref):
    tokens, channels = gated_ref.shape
    chunks = tokens // CHUNK
    offsets = lax.broadcasted_iota(jnp.int32, (CHUNK, channels), 0).astype(jnp.float32) - (CHUNK - 1) / 2.0
    rows = lax.broadcasted_iota(jnp.int32, (CHUNK, CHUNK), 0)
    cols = lax.broadcasted_iota(jnp.int32, (CHUNK, CHUNK), 1)
    tri = (rows >= cols).astype(jnp.float32).astype(jnp.bfloat16)
    intra_ref[...] = jnp.zeros_like(intra_ref)

    def add_mode(mode, unused):
        rate = decay_ref[mode]
        weight = mixing_ref[mode] * jnp.sqrt(rate)
        up = jnp.exp(offsets * rate)
        down = jnp.exp(-offsets * rate)
        for chunk in range(chunks):
            rows_of = pl.ds(chunk * CHUNK, CHUNK)
            high, low = bf16_split(up * gated_ref[rows_of, :])
            summed = jnp.dot(tri, high, preferred_element_type=jnp.float32) + jnp.dot(
                tri, low, preferred_element_type=jnp.float32
            )
            states = down * summed
            intra_ref[rows_of, :] += weight * states
        return unused

    lax.fori_loop(0, decay_ref.shape[0], add_mode, 0)


def front_kernel(feat_ref, halo_ref, taps_ref, decay_ref, first_ref, gated_ref, ends_ref, ext_ref):
    tokens, channels = first_ref.shape
    chunks = tokens // CHUNK
    lead = 8

    def short(stream, rows_of):
        taps = [taps_ref[stream, pl.ds(offset, 1), :] for offset in range(TAPS)]
        total = taps[0] * ext_ref[stream, pl.ds(lead + rows_of, CHUNK), :]
        for offset in range(1, TAPS):
            total = total + taps[offset] * ext_ref[stream, pl.ds(lead - offset + rows_of, CHUNK), :]
        return total

    for stream in range(3):
        cols = pl.ds(stream * channels, channels)
        ext_ref[stream, pl.ds(lead - (TAPS - 1), TAPS - 1), :] = halo_ref[:, cols].astype(jnp.float32)
        ext_ref[stream, pl.ds(lead, tokens), :] = feat_ref[:, cols].astype(jnp.float32)
    for chunk in range(chunks):
        rows_of = chunk * CHUNK
        first_ref[pl.ds(rows_of, CHUNK), :] = short(0, rows_of)
        product = short(1, rows_of) * short(2, rows_of)
        gated_ref[pl.ds(rows_of, CHUNK), :] = product.astype(jnp.bfloat16).astype(jnp.float32)

    tail = (CHUNK - 1) - lax.broadcasted_iota(jnp.int32, (CHUNK, channels), 0).astype(jnp.float32)

    def add_mode(mode, unused):
        fade = jnp.exp(-tail * decay_ref[mode])
        for chunk in range(chunks):
            block = gated_ref[pl.ds(chunk * CHUNK, CHUNK), :]
            ends_ref[mode, pl.ds(chunk, 1), :] = jnp.sum(fade * block, axis=0, keepdims=True)
        return unused

    lax.fori_loop(0, decay_ref.shape[0], add_mode, 0)


def front_call(features, halo, short_filter, decay3):
    tokens, streams, channels = features.shape
    modes = decay3.shape[0]
    chunks = tokens // CHUNK
    return pl.pallas_call(
        front_kernel,
        out_shape=(
            whole((tokens, channels), jnp.float32),
            whole((tokens, channels), jnp.float32),
            whole((modes, chunks, channels), jnp.float32),
        ),
        in_specs=in_vmem(4),
        out_specs=tuple(in_vmem(3)),
        scratch_shapes=[pltpu.VMEM((streams, tokens + 8, channels), jnp.float32)],
        cost_estimate=pl.CostEstimate(
            flops=2 * (3 * TAPS + modes) * tokens * channels, transcendentals=modes * CHUNK * channels,
            bytes_accessed=14 * tokens * channels,
        ),
    )(features.reshape(tokens, streams * channels), halo.reshape(halo.shape[0], streams * channels), short_filter, decay3)


def finish_kernel(intra_ref, state_ref, decay_ref, mixing_ref, gated_ref, first_ref, skip_ref, mixer_ref, acc_ref):
    tokens, channels = gated_ref.shape
    chunks = tokens // CHUNK
    after = lax.broadcasted_iota(jnp.int32, (CHUNK, channels), 0).astype(jnp.float32) + 1.0
    acc_ref[...] = intra_ref[...]

    def add_mode(mode, unused):
        rate = decay_ref[mode]
        decayed = jnp.exp(-after * rate) * (mixing_ref[mode] * jnp.sqrt(rate))
        for chunk in range(chunks):
            rows_of = pl.ds(chunk * CHUNK, CHUNK)
            acc_ref[rows_of, :] += decayed * state_ref[mode, pl.ds(chunk, 1), :]
        return unused

    lax.fori_loop(0, decay_ref.shape[0], add_mode, 0)
    filtered = acc_ref[...] + skip_ref[...] * gated_ref[...]
    filtered = filtered.astype(jnp.bfloat16).astype(jnp.float32)
    mixer_ref[...] = (first_ref[...] * filtered).astype(mixer_ref.dtype)


def whole(shape, dtype):
    return jax.ShapeDtypeStruct(shape, dtype)


def in_vmem(count):
    return [pl.BlockSpec(memory_space=pltpu.VMEM)] * count


def intra_call(gated, decay3, mixing3):
    tokens, channels = gated.shape
    modes = decay3.shape[0]
    return pl.pallas_call(
        intra_kernel,
        out_shape=whole((tokens, channels), jnp.float32),
        in_specs=in_vmem(3),
        out_specs=pl.BlockSpec(memory_space=pltpu.VMEM),
        cost_estimate=pl.CostEstimate(
            flops=4 * modes * tokens * CHUNK * channels, transcendentals=2 * modes * CHUNK * channels,
            bytes_accessed=8 * tokens * channels,
        ),
    )(gated, decay3, mixing3)


def exchange_history(block_end, decay, tok_dev):
    count = lax.axis_size("ctx")
    group = math.gcd(count, GROUP)
    me = lax.axis_index("ctx")
    place = me % group

    def decayed(blocks):
        return jnp.exp(-(blocks.astype(jnp.float32) * float(tok_dev)) * decay)

    prefix = jnp.zeros_like(decay)
    total = decayed(group - 1 - place) * block_end
    for shift in range(1, group):
        pairs = [(g + q, g + (q + shift) % group) for g in range(0, count, group) for q in range(group)]
        arrived = lax.ppermute(block_end, "ctx", pairs)
        source = (place - shift) % group
        prefix = prefix + jnp.where(source < place, decayed(place - 1 - source), 0.0) * arrived
        total = total + decayed(group - 1 - source) * arrived
    entering = jnp.zeros_like(decay)
    for hop in range(1, count // group):
        arrived = from_behind(total, "ctx", hop * group)
        entering = entering + decayed(jnp.int32((hop - 1) * group)) * arrived
    return prefix + decayed(place) * entering


def finish_call(intra, entering, decay3, mixing3, gated, first, skip):
    tokens, channels = gated.shape
    modes = decay3.shape[0]
    return pl.pallas_call(
        finish_kernel,
        out_shape=whole((tokens, channels), jnp.bfloat16),
        in_specs=in_vmem(7),
        out_specs=pl.BlockSpec(memory_space=pltpu.VMEM),
        scratch_shapes=[pltpu.VMEM((tokens, channels), jnp.float32)],
        cost_estimate=pl.CostEstimate(
            flops=2 * modes * tokens * channels, transcendentals=modes * CHUNK * channels,
            bytes_accessed=14 * tokens * channels,
        ),
    )(intra, entering, decay3, mixing3, gated, first, skip)


def chunk_states(ends, decay):
    step = jnp.exp(-float(CHUNK) * decay)
    carry = jnp.zeros_like(decay)
    entering = []
    for chunk in range(ends.shape[1]):
        entering.append(carry)
        carry = step * carry + ends[:, chunk]
    return jnp.stack(entering, axis=1), carry


def block_body(features, short_filter, decay_rate, residue, skip_gain, norm_gain, qkv_weight):
    tok_dev, _, channels = features.shape
    head_cols = qkv_weight.shape[2]
    shard_rows = lax.all_gather(qkv_weight, "ctx", axis=0, tiled=True)
    rim_rows = features[tok_dev - (TAPS - 1) :]
    before = from_behind(rim_rows, "ctx", 1)
    decay3 = decay_rate[:, None, :]
    mixing3 = residue[:, None, :]
    first, gated, ends = front_call(features, before, short_filter, decay3)
    entering, block_end = chunk_states(ends, decay_rate)
    history = exchange_history(block_end, decay_rate, tok_dev)
    intra = intra_call(gated, decay3, mixing3)
    chunks = tok_dev // CHUNK
    lead = jnp.exp(-float(CHUNK) * jnp.arange(chunks, dtype=jnp.float32)[None, :, None] * decay_rate[:, None, :])
    total_state = entering + lead * history[:, None, :]
    mixer = finish_call(intra, total_state, decay3, mixing3, gated, first, skip_gain[None])

    parts = lax.axis_size("tp")
    me = lax.axis_index("tp")
    pieces = [mixer] + [
        lax.ppermute(mixer, "tp", [((source + shift) % parts, source) for source in range(parts)])
        for shift in range(1, parts)
    ]
    doubled = jnp.concatenate(pieces + pieces, axis=1)
    gathered = lax.dynamic_slice_in_dim(doubled, ((parts - me) % parts) * channels, parts * channels, 1)
    as_float = gathered.astype(jnp.float32)
    inverse = lax.rsqrt(jnp.mean(as_float * as_float, axis=1, keepdims=True) + EPSILON)
    normed = (as_float * inverse * norm_gain[None]).astype(jnp.bfloat16)
    flat_rows = shard_rows.reshape(shard_rows.shape[0], 3 * head_cols)
    kv_pair = jnp.dot(normed, flat_rows[:, head_cols:], preferred_element_type=jnp.float32).astype(jnp.bfloat16)
    heads = head_cols // HD
    head_k = [[kv_pair[:, h * HD : (h + 1) * HD]] for h in range(heads)]
    head_v = [[kv_pair[:, head_cols + h * HD : head_cols + (h + 1) * HD]] for h in range(heads)]
    for _ in range(WINDOW - 1):
        for h in range(heads):
            head_k[h].append(from_behind(head_k[h][-1], "ctx", 1))
            head_v[h].append(from_behind(head_v[h][-1], "ctx", 1))
    blocks_k = [jnp.concatenate([head_k[h][lag] for h in range(heads)], axis=1) for lag in range(WINDOW)]
    blocks_v = [jnp.concatenate([head_v[h][lag] for h in range(heads)], axis=1) for lag in range(WINDOW)]
    projected_q = jnp.dot(normed, flat_rows[:, :head_cols], preferred_element_type=jnp.float32).astype(jnp.bfloat16)
    query = projected_q.reshape(tok_dev, heads, HD)
    position = lax.axis_index("ctx")
    row_ids = jnp.arange(tok_dev)
    causal = row_ids[:, None] >= row_ids[None, :]
    score_list = []
    for lag_step in range(WINDOW):
        keys = blocks_k[lag_step].reshape(tok_dev, heads, HD)
        scores = jnp.einsum(
            "thd,shd->hts", query, keys, preferred_element_type=jnp.float32
        ) / math.sqrt(HD)
        if lag_step == 0:
            allowed = causal
        else:
            allowed = jnp.broadcast_to(position >= lag_step, causal.shape)
        score_list.append(jnp.where(allowed[None], scores, -jnp.inf))
    peak = reduce(jnp.maximum, [jnp.max(entry, axis=2) for entry in score_list])
    total = jnp.zeros((heads, tok_dev), jnp.float32)
    output = jnp.zeros((tok_dev, heads, HD), jnp.float32)
    for lag_step in range(WINDOW):
        expo = jnp.exp(score_list[lag_step] - peak[:, :, None])
        total = total + jnp.sum(expo, axis=2)
        values = blocks_v[lag_step].reshape(tok_dev, heads, HD)
        output = output + jnp.einsum(
            "hts,shd->thd", expo.astype(jnp.bfloat16), values, preferred_element_type=jnp.float32
        )
    attended = (output / total.T[:, :, None]).astype(jnp.bfloat16).reshape(tok_dev, head_cols)
    return (mixer, attended)


def solution(mesh):
    placed = (
        P("ctx", None, "tp"),
        P(None, None, "tp"),
        P(None, "tp"),
        P(None, "tp"),
        P("tp"),
        P(),
        P("ctx", None, "tp"),
    )
    return jax.shard_map(
        block_body,
        mesh=mesh,
        in_specs=placed,
        out_specs=(P("ctx", "tp"), P("ctx", "tp")),
        check_vma=False,
    )
```
